32 devices in a mesh: groups: 2 (over y), seq: 4 (over z), tp: 4 (over x, core).
Axes of the slice: x: 2, y: 2, z: 4, core: 2. Of those that a mesh axis runs over, the one named last changes fastest.
Arguments:
- activations: bfloat16 [1024, 8192], P(('groups', 'seq'), 'tp'), parts along dimension 0, may hold values from -24 to 24
- queries: bfloat16 [1024, 8192], P(('groups', 'seq'), 'tp'), parts along dimension 0, may hold values from -24 to 24
- key_weight: bfloat16 [8192, 1024], P(None, 'tp'), may hold values from -0.0625 to 0.0625
- value_weight: bfloat16 [8192, 1024], P(None, 'tp'), may hold values from -0.0625 to 0.0625
- lengths: int32 [8], P('groups'), parts along dimension 0, may hold values from 1 to 320, 512 in all
- owners: int32 [32], P('groups'), parts along dimension 0, may hold values from 0 to 3, as said below
Outputs:
- attention: bfloat16 [1024, 8192], P(('groups', 'seq'), 'tp'), parts along dimension 0
- kv_cache: bfloat16 [1024, 8, 256], P(('groups', 'seq'), 'tp'), parts along dimension 0
The draws below stay inside these ranges and needn't reach their ends.
There are 2 independent parts, one for each index of `groups`. The reference program is written for one: setup_inputs(seed, part) draws one part's arguments, and reference() takes and returns one part's arrays. A program takes and returns all parts, laid end to end along the dimension named above; an argument that names none is the same for every part. Nothing has to cross between parts.
Inputs may be any that keep to these rules, and one draw needn't show every extreme that they name: `owners`: every decode device is named by exactly 4 blocks; among the 4 blocks of the rows of one index of seq, no decode device is named more than 2 times, and some is named exactly 2 times.
All inputs are finite; a program needn't handle non-finite values.
Results may differ from the reference program's by a relative error of at most 0.0045.
The reference program's roundings to bfloat16 on the way count: a program that leaves them out, or rounds other values in their place, can miss the bound.
Values may be sent and summed in bfloat16 or wider, within the bound.
No kernel may reach another device: no remote copies, remote signals or barrier semaphores. Data moves between devices by JAX's collectives and lax.ppermute only.
A program may use at most 64 MiB of HBM per device.

```python
import math
import jax
import jax.numpy as jnp
import numpy as np
from jax import lax

D = 8192
QH = 64
KVH = 8
HD = 128
PROMPTS = 4
TOK_DEV = 128
TOKENS = 512
LONGEST = 320
BLOCK = 32
BLOCKS = 16


def scaled_normal(key, row_count, col_count):
    sample = jax.random.normal(jax.random.fold_in(key, 3), (row_count, col_count), jnp.float32)
    return jnp.clip(sample, -24.0, 24.0)


def draw_activations(key, part):
    return scaled_normal(key, TOKENS, D).astype(jnp.bfloat16)


def draw_queries(key, part):
    return scaled_normal(key, TOKENS, QH * HD).astype(jnp.bfloat16)


def draw_owners(key, part):
    per_source = TOK_DEV // BLOCK
    sources = BLOCKS // per_source
    doubled = max(1, per_source // 4)
    base_perm = jax.random.permutation(jax.random.fold_in(key, 21), per_source)
    within = jnp.arange(per_source)
    pattern = jnp.where((within >= doubled) & (within < 2 * doubled), base_perm[jnp.maximum(within - doubled, 0)], base_perm)
    shifted = jax.random.permutation(jax.random.fold_in(key, 22), sources)
    subkeys = jax.random.split(jax.random.fold_in(key, 23), sources)
    mixes = jax.vmap(lambda subkey: jax.random.permutation(subkey, per_source))(subkeys)
    owner_table = (pattern[mixes] + shifted[:, None]) % sources
    return owner_table.reshape(BLOCKS).astype(jnp.int32)


def block_levels(own_key, extent, cuts, least, top_value):
    def one(position, shards_of):
        draws = jax.random.uniform(jax.random.fold_in(jax.random.fold_in(own_key, 6), position), (shards_of,), jnp.float32, least / len(cuts), top_value / len(cuts))
        return jnp.repeat(jnp.exp(draws), extent[position] // shards_of).reshape((-1,) + (1,) * (len(extent) - position - 1))

    gain = one(*cuts[0])
    for cut in cuts[1:]:
        gain = gain * one(*cut)
    return gain


def profile(count, total, limit, skew):
    loads = [(1 << 20) // math.isqrt(grade ** skew) + 1 for grade in range(2, count + 1)]
    rest, given = total - limit - (count - 1), [1] * (count - 1)
    while rest > 0:
        candidates = [i for i in range(count - 1) if given[i] < limit]
        whole, budget = sum([loads[i] for i in candidates]), rest
        for i in candidates:
            addition = min(limit - given[i], max(1, budget * loads[i] // whole), rest)
            given[i] = given[i] + addition
            rest = rest - addition
    return np.array([limit] + given)


def ragged(rng, number_of, total, reach, lean):
    if number_of == 2:
        one = jax.random.randint(rng, (), max(1, total - reach), min(reach, total - 1) + 1)
        return jnp.stack([one, total - one])
    sizes = jnp.asarray(profile(number_of, total, reach, lean), jnp.int32)
    pairs = (number_of - 1) // 2
    donor, sink = sizes[1:1 + 2 * pairs:2], sizes[2:2 + 2 * pairs:2]
    room = jnp.minimum(donor - 1, reach - sink)
    moved = jax.random.randint(jax.random.fold_in(rng, 1), (pairs,), 0, 1 << 20) % (room + 1)
    sizes = sizes.at[1:1 + 2 * pairs:2].set(donor - moved).at[2:2 + 2 * pairs:2].set(sink + moved)
    return sizes[jax.random.permutation(jax.random.fold_in(rng, 2), number_of)]


def bell_draw(rng, dims, deviation, most, pieces=(), kind=jnp.bfloat16):
    loudness = block_levels(rng, dims, pieces, -0.22, 0.18) if pieces else 1.0
    drawn = jax.random.normal(rng, dims, jnp.float32) * deviation * loudness
    return jnp.minimum(jnp.maximum(drawn, -most), most).astype(kind)


def setup_inputs(seed: int = 0, part: int = 0) -> dict:
    key_list = jax.random.split(jax.random.key(seed), 7)
    part_keys = jax.random.split(jax.random.fold_in(key_list[6], part), 7)
    activations = draw_activations(jax.random.fold_in(jax.random.fold_in(key_list[6], part), 71), part)
    queries = draw_queries(jax.random.fold_in(jax.random.fold_in(key_list[6], part), 71), part)
    key_weight = bell_draw(key_list[2], (D, KVH * HD), D ** -0.5, 0.0625, ((1, 4),))
    value_weight = bell_draw(key_list[3], (D, KVH * HD), D ** -0.5, 0.0625, ((1, 4),))
    lengths = ragged(part_keys[4], PROMPTS, TOKENS, LONGEST, 2).astype(jnp.int32)
    owners = draw_owners(jax.random.fold_in(jax.random.fold_in(key_list[6], part), 71), part)
    return dict(activations=activations, queries=queries, key_weight=key_weight, value_weight=value_weight, lengths=lengths, owners=owners)


def locate(row_ids, lengths):
    prompt_ends = jnp.cumsum(lengths).astype(jnp.int32)
    prompt_starts = (prompt_ends - lengths).astype(jnp.int32)
    segment = lax.optimization_barrier(jnp.sum((row_ids[:, None] >= prompt_ends[None, :]).astype(jnp.int32), axis=1)).astype(jnp.int32)
    numbers = jnp.arange(lengths.shape[0], dtype=jnp.int32)
    prompt_first = lax.optimization_barrier(jnp.sum(jnp.where(segment[:, None] == numbers[None, :], prompt_starts[None, :], 0), axis=1)).astype(jnp.int32)
    return (segment, (row_ids - prompt_first).astype(jnp.int32))

def rotate(vectors, positions):
    half_size = vectors.shape[-1] // 2
    exponent = jnp.arange(half_size, dtype=jnp.float32) * (2.0 / vectors.shape[-1])
    inverse = jnp.exp(-exponent * jnp.log(jnp.float32(500000.0)))
    angles = positions.astype(jnp.float32)[:, None] * inverse[None, :]
    cosines = jnp.cos(angles)[:, None, :]
    sine_values = jnp.sin(angles)[:, None, :]
    lower_half = vectors[..., :half_size]
    upper_half = vectors[..., half_size:]
    return jnp.concatenate([lower_half * cosines - upper_half * sine_values, upper_half * cosines + lower_half * sine_values], axis=-1)

def reference(activations, queries, key_weight, value_weight, lengths, owners):
    row_ids = jnp.arange(TOKENS, dtype=jnp.int32)
    segment, positions = locate(row_ids, lengths)
    key_sums = jnp.dot(activations, key_weight, preferred_element_type=jnp.float32)
    keys_local = rotate(key_sums.reshape(TOKENS, KVH, HD), positions).astype(jnp.bfloat16)
    values_local = jnp.dot(activations, value_weight, preferred_element_type=jnp.float32).astype(jnp.bfloat16).reshape(TOKENS, KVH, HD)
    rotated = rotate(queries.astype(jnp.float32).reshape(TOKENS, QH, HD), positions).astype(jnp.bfloat16)
    group_size = QH // KVH
    block_size = 512 if TOKENS % 512 == 0 else TOKENS
    query_blocks = rotated.reshape(TOKENS // block_size, block_size, KVH, group_size, HD)
    block_ids = row_ids.reshape(TOKENS // block_size, block_size)

    def one_block(carried):
        query_block, block_rows = carried
        allowed = (segment[block_rows][:, None] == segment[None, :]) & (row_ids[None, :] <= block_rows[:, None])

        def one_head(kv_index):
            query_part = lax.dynamic_index_in_dim(query_block, kv_index, 1, keepdims=False).astype(jnp.float32)
            key_part = lax.dynamic_index_in_dim(keys_local, kv_index, 1, keepdims=False).astype(jnp.float32)
            value_part = lax.dynamic_index_in_dim(values_local, kv_index, 1, keepdims=False).astype(jnp.float32)
            scores = jnp.einsum('sgd,td->sgt', query_part, key_part) / jnp.sqrt(jnp.float32(HD))
            mask_wide = allowed[:, None, :]
            largest = lax.optimization_barrier(jnp.max(jnp.where(mask_wide, scores, -jnp.inf), axis=-1, keepdims=True))
            weights = jnp.where(mask_wide, jnp.exp(scores - largest), 0.0)
            totals = lax.optimization_barrier(jnp.sum(weights, axis=-1, keepdims=True))
            rounded = lax.optimization_barrier(weights.astype(jnp.bfloat16)).astype(jnp.float32)
            return jnp.einsum('sgt,td->sgd', rounded, value_part) / totals
        per_head = lax.map(one_head, jnp.arange(KVH, dtype=jnp.int32))
        return jnp.transpose(per_head, (1, 0, 2, 3)).reshape(block_size, QH * HD).astype(jnp.bfloat16)
    attention = lax.map(one_block, (query_blocks, block_ids)).reshape(TOKENS, QH * HD)
    paired = jnp.concatenate([keys_local, values_local], axis=-1)
    blocks = paired.reshape(BLOCKS, BLOCK, KVH, 2 * HD)
    ordering = jnp.argsort(owners, stable=True)
    kv_cache = blocks[ordering].reshape(TOKENS, KVH, 2 * HD)
    return (attention, kv_cache)
```

```python
import jax
import jax.numpy as jnp
from jax import lax
from jax.sharding import PartitionSpec as P

HD = 128


def locate(row_ids, lengths):
    prompt_ends = jnp.cumsum(lengths)
    prompt_starts = prompt_ends - lengths
    segment = jnp.sum((row_ids[:, None] >= prompt_ends[None, :]).astype(jnp.int32), axis=1)
    numbers = jnp.arange(lengths.shape[0], dtype=jnp.int32)
    prompt_first = jnp.sum(
        jnp.where(segment[:, None] == numbers[None, :], prompt_starts[None, :], 0), axis=1
    )
    return (segment, row_ids - prompt_first)


def rotate(vectors, positions):
    half_size = vectors.shape[-1] // 2
    exponent = jnp.arange(half_size, dtype=jnp.float32) * (2.0 / vectors.shape[-1])
    inverse = jnp.exp(-exponent * jnp.log(jnp.float32(500000.0)))
    angles = positions.astype(jnp.float32)[:, None] * inverse[None, :]
    cosines = jnp.cos(angles)[:, None, :]
    sine_values = jnp.sin(angles)[:, None, :]
    lower_half = vectors[..., :half_size]
    upper_half = vectors[..., half_size:]
    return jnp.concatenate(
        [
            lower_half * cosines - upper_half * sine_values,
            upper_half * cosines + lower_half * sine_values,
        ],
        axis=-1,
    )


def swap(array, axis, distance):
    count = lax.axis_size(axis)
    return lax.ppermute(array, axis, [(i, i ^ distance) for i in range(count)])


def is_power(count):
    return count & (count - 1) == 0


def split_rows(rows):
    half = rows // 2
    return [(0, half), (half, rows - half)] if half % 16 == 0 and half else [(0, rows)]


def project(activations, weights, chunks):
    parts = lax.axis_size("tp")
    own = lax.axis_index("tp")
    width = activations.shape[1]

    def rows_of(offset):
        return lax.dynamic_slice_in_dim(weights, (own ^ offset) * width, width, 0)

    pieces = {c: {0: activations[start : start + size]} for c, (start, size) in enumerate(chunks)}
    distance = parts // 2
    while distance:
        for c in pieces:
            for offset in list(pieces[c]):
                pieces[c][offset ^ distance] = swap(pieces[c][offset], "tp", distance)
        distance //= 2
    sums = []
    for c in pieces:
        total = None
        for offset in sorted(pieces[c]):
            term = jnp.dot(pieces[c][offset], rows_of(offset), preferred_element_type=jnp.float32)
            total = term if total is None else total + term
        sums.append(total)
    return sums


def per_device(activations, queries, key_weight, value_weight, lengths, owners):
    local_rows = activations.shape[0]
    devices = lax.axis_size("seq")
    own_index = lax.axis_index("seq")
    kv_width = key_weight.shape[1]
    kv_heads = kv_width // HD
    query_heads = queries.shape[1] // HD
    group_size = query_heads // kv_heads
    row_ids = own_index * local_rows + jnp.arange(local_rows, dtype=jnp.int32)
    segment, positions = locate(row_ids, lengths)
    chunks = split_rows(local_rows)
    weights = jnp.concatenate([key_weight, value_weight], axis=1)
    arrived = []
    for (start, size), sums in zip(chunks, project(activations, weights, chunks)):
        keys_local = rotate(
            sums[:, :kv_width].reshape(size, kv_heads, HD), positions[start : start + size]
        ).astype(jnp.bfloat16)
        values_local = sums[:, kv_width:].astype(jnp.bfloat16).reshape(size, kv_heads, HD)
        packed = jnp.concatenate([keys_local, values_local], axis=-1).reshape(
            size, kv_heads * 2 * HD
        )
        by_offset = [packed] + [swap(packed, "seq", k) for k in range(1, devices)]
        arrived.append(by_offset)
    by_offset = [jnp.concatenate([part[k] for part in arrived], axis=0) for k in range(devices)]
    stacked = jnp.stack(by_offset, axis=0)
    order = own_index ^ jnp.arange(devices, dtype=jnp.int32)
    key_row_ids = (
        order[:, None] * local_rows + jnp.arange(local_rows, dtype=jnp.int32)[None, :]
    ).reshape(-1)
    rotated = rotate(queries.astype(jnp.float32).reshape(local_rows, query_heads, HD), positions)
    rotated = rotated.astype(jnp.bfloat16).reshape(local_rows, kv_heads, group_size, HD)

    def attend_block(running, portion, offset):
        running_max, running_sum, running_out = running
        amount = portion.shape[0]
        paired = portion.reshape(amount, kv_heads, 2 * HD)
        key_part = paired[:, :, :HD]
        value_part = paired[:, :, HD:]
        key_rows = offset
        key_segment, unused = locate(key_rows, lengths)
        allowed = (
            (key_segment[None, :] == segment[:, None])
            & (key_rows[None, :] <= row_ids[:, None])
            & (key_rows[None, :] >= 0)
        )
        allowed = allowed[:, None, None, :]
        scores = jnp.einsum(
            "qhgd,khd->qhgk", rotated, key_part, preferred_element_type=jnp.float32
        ) / jnp.sqrt(jnp.float32(HD))
        new_max = jnp.maximum(running_max, jnp.max(jnp.where(allowed, scores, -1e30), axis=-1))
        weights = jnp.where(allowed, jnp.exp(scores - new_max[..., None]), 0.0)
        factor = jnp.exp(running_max - new_max)
        running_sum = running_sum * factor + jnp.sum(weights, axis=-1)
        running_out = running_out * factor[..., None] + jnp.einsum(
            "qhgk,khd->qhgd",
            weights.astype(jnp.bfloat16),
            value_part,
            preferred_element_type=jnp.float32,
        )
        return (new_max, running_sum, running_out)

    initial = (
        jnp.full((local_rows, kv_heads, group_size), -1e30, jnp.float32),
        jnp.zeros((local_rows, kv_heads, group_size), jnp.float32),
        jnp.zeros((local_rows, kv_heads, group_size, HD), jnp.float32),
    )
    blocks_dev = owners.shape[0] // devices
    block_len = local_rows // blocks_dev
    is_own = owners == own_index
    ordinal = jnp.cumsum(is_own.astype(jnp.int32)) - 1
    matches = is_own[None, :] & (
        ordinal[None, :] == jnp.arange(blocks_dev, dtype=jnp.int32)[:, None]
    )
    leading = jnp.sum(
        jnp.where(matches, jnp.arange(owners.shape[0], dtype=jnp.int32)[None, :], 0), axis=1
    )
    within = jnp.arange(local_rows, dtype=jnp.int32)
    wanted = jnp.repeat(leading, block_len) * block_len + within % block_len
    portion = stacked.reshape(devices * local_rows, -1)
    choose = (wanted[:, None] == key_row_ids[None, :]).astype(jnp.bfloat16)
    running = attend_block(initial, portion, key_row_ids)
    taken = jnp.dot(choose, portion, preferred_element_type=jnp.float32)
    kv_cache = taken.astype(jnp.bfloat16).reshape(local_rows, kv_heads, 2 * HD)
    running_max, running_sum, running_out = running
    attention = (
        (running_out / running_sum[..., None])
        .astype(jnp.bfloat16)
        .reshape(local_rows, query_heads * HD)
    )
    return (attention, kv_cache)


def solution(mesh):
    in_specs = (
        P(("groups", "seq"), "tp"),
        P(("groups", "seq"), "tp"),
        P(None, "tp"),
        P(None, "tp"),
        P("groups"),
        P("groups"),
    )
    out_specs = (P(("groups", "seq"), "tp"), P(("groups", "seq"), "tp", None))
    return jax.shard_map(
        per_device, mesh=mesh, in_specs=in_specs, out_specs=out_specs, check_vma=False
    )
```

```python
import functools

import jax
import jax.numpy as jnp
import numpy as np
from jax import lax
from jax.experimental import pallas as pl
from jax.experimental.pallas import tpu as pltpu
from jax.sharding import PartitionSpec as P

HD = 128
LOW = -1e30
MIB = 1 << 20
VMEM = pl.BlockSpec(memory_space=pltpu.VMEM)
SMEM = pl.BlockSpec(memory_space=pltpu.SMEM)


def locate(row_ids, lengths):
    prompt_ends = jnp.cumsum(lengths)
    prompt_starts = prompt_ends - lengths
    segment = jnp.sum((row_ids[:, None] >= prompt_ends[None, :]).astype(jnp.int32), axis=1)
    numbers = jnp.arange(lengths.shape[0], dtype=jnp.int32)
    prompt_first = jnp.sum(
        jnp.where(segment[:, None] == numbers[None, :], prompt_starts[None, :], 0), axis=1
    )
    return (segment, row_ids - prompt_first)


def rotate(vectors, positions):
    half_size = vectors.shape[-1] // 2
    exponent = jnp.arange(half_size, dtype=jnp.float32) * (2.0 / vectors.shape[-1])
    inverse = jnp.exp(-exponent * jnp.log(jnp.float32(500000.0)))
    angles = positions.astype(jnp.float32)[:, None] * inverse[None, :]
    cosines = jnp.cos(angles)[:, None, :]
    sine_values = jnp.sin(angles)[:, None, :]
    lower_half = vectors[..., :half_size]
    upper_half = vectors[..., half_size:]
    return jnp.concatenate(
        [
            lower_half * cosines - upper_half * sine_values,
            upper_half * cosines + lower_half * sine_values,
        ],
        axis=-1,
    )


def swap(array, axis, distance):
    count = lax.axis_size(axis)
    return lax.ppermute(array, axis, [(i, i ^ distance) for i in range(count)])


def is_power(count):
    return count & (count - 1) == 0


def call(body, out_shape, in_specs, vmem=8 * MIB, scratch=(), out_specs=None):
    multiple = isinstance(out_shape, (list, tuple))
    return pl.pallas_call(
        body,
        out_shape=out_shape,
        in_specs=in_specs,
        out_specs=out_specs or ([VMEM] * len(out_shape) if multiple else VMEM),
        scratch_shapes=list(scratch),
        compiler_params=pltpu.CompilerParams(vmem_limit_bytes=vmem),
    )


def first_rows(rows, lengths_ref):
    first = jnp.zeros_like(rows)
    start = jnp.int32(0)
    for p in range(lengths_ref.shape[0]):
        first = jnp.where(rows >= start, start, first)
        start = start + lengths_ref[p]
    return first


def turn(vectors, cosines, sines):
    return vectors * cosines + pltpu.roll(vectors, HD // 2, 1) * sines


def prepare_body(place_ref, lengths_ref, inverse_ref, queries_ref, cos_ref, sin_ref, rotated_ref):
    local_rows, width = queries_ref.shape
    rows = place_ref[0] * local_rows + lax.broadcasted_iota(jnp.int32, (local_rows, HD), 0)
    positions = rows - first_rows(rows, lengths_ref)
    angles = positions.astype(jnp.float32) * inverse_ref[...]
    lanes = lax.broadcasted_iota(jnp.int32, (local_rows, HD), 1)
    cosines = jnp.cos(angles)
    sines = jnp.sin(angles)
    sines = jnp.where(lanes < HD // 2, -sines, sines)
    cos_ref[...] = cosines
    sin_ref[...] = sines
    for h in range(width // HD):
        vectors = queries_ref[:, h * HD : (h + 1) * HD].astype(jnp.float32)
        rotated_ref[:, h * HD : (h + 1) * HD] = turn(vectors, cosines, sines).astype(jnp.bfloat16)


def products(pieces, offsets, place_ref, key_ref, value_ref):
    keys = values = None
    for ref, offset in zip(pieces, offsets):
        width = ref.shape[1]
        start = pl.multiple_of((place_ref[1] ^ offset) * width, width)
        piece = ref[...]
        key_term = jnp.dot(
            piece, key_ref[pl.ds(start, width), :], preferred_element_type=jnp.float32
        )
        value_term = jnp.dot(
            piece, value_ref[pl.ds(start, width), :], preferred_element_type=jnp.float32
        )
        keys = key_term if keys is None else keys + key_term
        values = value_term if values is None else values + value_term
    return keys, values


def early_body(offsets, place_ref, key_ref, value_ref, *refs):
    key_sums_ref, value_sums_ref = refs[-2:]
    keys, values = products(refs[:-2], offsets, place_ref, key_ref, value_ref)
    key_sums_ref[...] = keys
    value_sums_ref[...] = values


def late_body(
    offsets, start, place_ref, key_ref, value_ref, key_sums_ref, value_sums_ref, cos_ref, sin_ref, *refs
):
    packed_ref = refs[-1]
    size = packed_ref.shape[0]
    rows = slice(start, start + size)
    keys, values = products(refs[:-1], offsets, place_ref, key_ref, value_ref)
    keys = keys + key_sums_ref[rows, :]
    values = values + value_sums_ref[rows, :]
    cosines = cos_ref[rows, :]
    sines = sin_ref[rows, :]
    for h in range(keys.shape[1] // HD):
        part = slice(h * HD, (h + 1) * HD)
        base = 2 * h * HD
        packed_ref[:, base : base + HD] = turn(keys[:, part], cosines, sines).astype(jnp.bfloat16)
        packed_ref[:, base + HD : base + 2 * HD] = values[:, part].astype(jnp.bfloat16)


def gathered_device(activations, queries, key_weight, value_weight, lengths, owners):
    local_rows = activations.shape[0]
    devices = lax.axis_size("seq")
    own_index = lax.axis_index("seq")
    kv_width = key_weight.shape[1]
    kv_heads = kv_width // HD
    query_heads = queries.shape[1] // HD
    group_size = query_heads // kv_heads
    row_ids = own_index * local_rows + jnp.arange(local_rows, dtype=jnp.int32)
    segment, positions = locate(row_ids, lengths)
    portion = lax.all_gather(activations, "tp", axis=1, tiled=True)
    key_rows = key_weight
    key_sums = jnp.dot(portion, key_rows, preferred_element_type=jnp.float32)
    value_sums = jnp.dot(portion, value_weight, preferred_element_type=jnp.float32)
    keys_local = rotate(key_sums.reshape(local_rows, kv_heads, HD), positions).astype(jnp.bfloat16)
    values_local = value_sums.astype(jnp.bfloat16).reshape(local_rows, kv_heads, HD)
    packed = jnp.concatenate([keys_local, values_local], axis=-1).reshape(
        local_rows, kv_heads * 2 * HD
    )
    rotated = rotate(queries.astype(jnp.float32).reshape(local_rows, query_heads, HD), positions)
    rotated = rotated.astype(jnp.bfloat16).reshape(local_rows, kv_heads, group_size, HD)

    def attend_block(running, portion, offset):
        running_max, running_sum, running_out = running
        amount = portion.shape[0]
        paired = portion.reshape(amount, kv_heads, 2 * HD)
        key_part = paired[:, :, :HD]
        value_part = paired[:, :, HD:]
        key_rows = offset + jnp.arange(amount, dtype=jnp.int32)
        key_segment, _ = locate(key_rows, lengths)
        allowed = (
            (key_segment[None, :] == segment[:, None])
            & (key_rows[None, :] <= row_ids[:, None])
            & (key_rows[None, :] >= 0)
        )
        allowed = allowed[:, None, None, :]
        scores = jnp.einsum(
            "qhgd,khd->qhgk", rotated, key_part, preferred_element_type=jnp.float32
        ) / jnp.sqrt(jnp.float32(HD))
        new_max = jnp.maximum(running_max, jnp.max(jnp.where(allowed, scores, -1e30), axis=-1))
        weights = jnp.where(allowed, jnp.exp(scores - new_max[..., None]), 0.0)
        factor = jnp.exp(running_max - new_max)
        running_sum = running_sum * factor + jnp.sum(weights, axis=-1)
        running_out = running_out * factor[..., None] + jnp.einsum(
            "qhgk,khd->qhgd",
            weights.astype(jnp.bfloat16),
            value_part,
            preferred_element_type=jnp.float32,
        )
        return (new_max, running_sum, running_out)

    def attend(running, portion, offset):
        amount = portion.shape[0]
        if amount > 512 and amount % 512 == 0:

            def advance(carried, entry):
                sub_portion, sub_offset = entry
                return (attend_block(carried, sub_portion, offset + sub_offset), None)

            offsets = jnp.arange(amount // 512, dtype=jnp.int32) * 512
            running, _ = lax.scan(
                advance, running, (portion.reshape(amount // 512, 512, portion.shape[1]), offsets)
            )
            return running
        return attend_block(running, portion, offset)

    initial = (
        jnp.full((local_rows, kv_heads, group_size), -1e30, jnp.float32),
        jnp.zeros((local_rows, kv_heads, group_size), jnp.float32),
        jnp.zeros((local_rows, kv_heads, group_size, HD), jnp.float32),
    )
    blocks_dev = owners.shape[0] // devices
    block_len = local_rows // blocks_dev
    is_own = owners == own_index
    ordinal = jnp.cumsum(is_own.astype(jnp.int32)) - 1
    matches = is_own[None, :] & (
        ordinal[None, :] == jnp.arange(blocks_dev, dtype=jnp.int32)[:, None]
    )
    leading = jnp.sum(
        jnp.where(matches, jnp.arange(owners.shape[0], dtype=jnp.int32)[None, :], 0), axis=1
    )
    within = jnp.arange(local_rows, dtype=jnp.int32)
    wanted = jnp.repeat(leading, block_len) * block_len + within % block_len
    portion = lax.all_gather(packed, "seq", axis=0, tiled=True)
    amount = portion.shape[0]
    choose = (wanted[:, None] == jnp.arange(amount, dtype=jnp.int32)[None, :]).astype(jnp.bfloat16)
    running = attend(
        (initial, jnp.zeros((local_rows, packed.shape[1]), jnp.float32))[0], portion, jnp.int32(0)
    )
    taken = jnp.dot(choose, portion, preferred_element_type=jnp.float32)
    kv_cache = taken.astype(jnp.bfloat16).reshape(local_rows, kv_heads, 2 * HD)
    _, running_sum, running_out = running
    attention = (
        (running_out / running_sum[..., None])
        .astype(jnp.bfloat16)
        .reshape(local_rows, query_heads * HD)
    )
    return (attention, kv_cache)


def attend_body(starts, carried, final, place_ref, lengths_ref, owners_ref, rotated_ref, *refs):
    local_rows, width = rotated_ref.shape
    own = place_ref[0]
    devices = place_ref.shape[0] - 2
    chunks = len(starts) if final else 1
    groups = [refs[c * devices : (c + 1) * devices] for c in range(chunks)]
    rest = refs[chunks * devices :]
    if carried:
        old_max_ref, old_sum_ref, old_out_ref = rest[:3]
        rest = rest[3:]
    parts = groups[-1]
    size = parts[0].shape[0]
    amount = devices * size
    columns = lax.broadcasted_iota(jnp.int32, (local_rows, amount), 1)
    rows = own * local_rows + lax.broadcasted_iota(jnp.int32, (local_rows, amount), 0)
    key_rows = columns + ((own * local_rows) + starts[-1])
    for k in range(1, devices):
        base = (own ^ k) * local_rows + (starts[-1] - k * size)
        key_rows = jnp.where(columns >= k * size, columns + base, key_rows)
    allowed = (key_rows >= first_rows(rows, lengths_ref)) & (key_rows <= rows)
    scale = float(HD) ** -0.5
    kv_heads = parts[0].shape[1] // (2 * HD)
    query_heads = width // HD
    group_size = query_heads // kv_heads
    for j in range(kv_heads):
        base = 2 * j * HD
        keys = jnp.concatenate([ref[:, base : base + HD] for ref in parts], axis=0)
        values = jnp.concatenate([ref[:, base + HD : base + 2 * HD] for ref in parts], axis=0)
        for h in range(j * group_size, (j + 1) * group_size):
            lanes = slice(h * HD, (h + 1) * HD)
            scores = lax.dot_general(
                rotated_ref[:, lanes],
                keys,
                (((1,), (1,)), ((), ())),
                preferred_element_type=jnp.float32,
            )
            scores = jnp.where(allowed, scores, LOW)
            largest = jnp.max(scores, axis=1, keepdims=True)
            if carried:
                old_max = old_max_ref[:, h : h + 1]
                largest = jnp.maximum(largest, old_max)
            weights = jnp.exp((scores - largest) * scale)
            total = jnp.sum(weights, axis=1, keepdims=True)
            out = jnp.dot(weights.astype(jnp.bfloat16), values, preferred_element_type=jnp.float32)
            if carried:
                factor = jnp.exp((old_max - largest) * scale)
                total = total + old_sum_ref[:, h : h + 1] * factor
                out = out + old_out_ref[:, lanes] * factor
            if final:
                rest[0][:, lanes] = (out / total).astype(jnp.bfloat16)
            else:
                rest[0][:, h : h + 1] = largest
                rest[1][:, h : h + 1] = total
                rest[2][:, lanes] = out
    if final:
        cache_ref, leading_ref = rest[1:]
        total_blocks = owners_ref.shape[0]
        blocks_dev = total_blocks // devices
        block_len = local_rows // blocks_dev
        count = jnp.int32(0)
        for b in range(total_blocks):
            hit = owners_ref[b] == own

            @pl.when(hit)
            def _(b=b, count=count):
                leading_ref[count] = b

            count = count + hit.astype(jnp.int32)
        for r in range(blocks_dev):
            block = leading_ref[r]
            distance = (block // blocks_dev) ^ own
            row = (block % blocks_dev) * block_len
            for group, start in zip(groups, starts):
                for k, ref in enumerate(group):
                    inside = (distance == k) & (row >= start) & (row < start + ref.shape[0])

                    @pl.when(inside)
                    def _(ref=ref, start=start, row=row, r=r):
                        source = pl.ds(pl.multiple_of(row - start, block_len), block_len)
                        cache_ref[r * block_len : (r + 1) * block_len, :] = ref[source, :]


def chunked_device(activations, queries, key_weight, value_weight, lengths, owners, sizes):
    local_rows, _ = activations.shape
    query_width = queries.shape[1]
    devices = lax.axis_size("seq")
    parts = lax.axis_size("tp")
    kv_width = key_weight.shape[1]
    query_heads = query_width // HD
    place = jnp.stack(
        [lax.axis_index("seq"), lax.axis_index("tp")] + [jnp.int32(0)] * devices
    ).astype(jnp.int32)
    starts = [sum(sizes[:c]) for c in range(len(sizes))]
    far = parts // 2
    reached = [{0: activations[at : at + size]} for at, size in zip(starts, sizes)]
    for held in reached:
        if far:
            held[far] = swap(held[0], "tp", far)
    near = {0: activations}
    distance = far // 2
    while distance:
        for offset in list(near):
            near[offset ^ distance] = swap(near[offset], "tp", distance)
        distance //= 2

    exponent = np.arange(HD // 2) * (2.0 / HD)
    inverse = np.exp(-exponent * np.log(500000.0)).astype(np.float32)
    inverse = jnp.asarray(np.concatenate([inverse, inverse])[None, :])
    table = jax.ShapeDtypeStruct((local_rows, HD), jnp.float32)
    cosines, sines, rotated = call(
        prepare_body,
        [table, table, jax.ShapeDtypeStruct(queries.shape, jnp.bfloat16)],
        [SMEM, SMEM, VMEM, VMEM],
    )(place, lengths, inverse, queries)
    offsets = sorted(near)
    sums = jax.ShapeDtypeStruct((local_rows, kv_width), jnp.float32)
    key_sums, value_sums = call(
        functools.partial(early_body, offsets), [sums, sums], [SMEM] + [VMEM] * (2 + len(offsets))
    )(place, key_weight, value_weight, *[near[o] for o in offsets])

    arrived = []
    ready = key_sums
    for held, start, size in zip(reached, starts, sizes):
        late = {far: lax.optimization_barrier((held[far], ready))[0]}
        distance = far // 2
        while distance:
            for offset in list(late):
                late[offset ^ distance] = swap(late[offset], "tp", distance)
            distance //= 2
        offsets = sorted(late)
        packed = call(
            functools.partial(late_body, offsets, start),
            jax.ShapeDtypeStruct((size, 2 * kv_width), jnp.bfloat16),
            [SMEM] + [VMEM] * (6 + len(offsets)),
        )(
            place,
            key_weight,
            value_weight,
            key_sums,
            value_sums,
            cosines,
            sines,
            *[late[o] for o in offsets],
        )
        ready = packed
        arrived.append([packed] + [swap(packed, "seq", k) for k in range(1, devices)])

    state = ()
    for c in range(len(sizes)):
        final = c == len(sizes) - 1
        groups = arrived if final else arrived[c : c + 1]
        taken = [part for group in groups for part in group]
        if final:
            results = [
                jax.ShapeDtypeStruct(queries.shape, jnp.bfloat16),
                jax.ShapeDtypeStruct((local_rows, 2 * kv_width), jnp.bfloat16),
            ]
        else:
            column = jax.ShapeDtypeStruct((local_rows, query_heads), jnp.float32)
            results = [column, column, jax.ShapeDtypeStruct(queries.shape, jnp.float32)]
        state = call(
            functools.partial(attend_body, tuple(starts[: c + 1]), c > 0, final),
            results,
            [SMEM] * 3 + [VMEM] * (1 + len(taken) + len(state)),
            scratch=[pltpu.SMEM((owners.shape[0] // devices,), jnp.int32)] if final else (),
        )(place, lengths, owners, rotated, *taken, *state)
    attention, cache = state
    return attention, cache.reshape(local_rows, kv_width // HD, 2 * HD)


def per_device(activations, queries, key_weight, value_weight, lengths, owners):
    local_rows = activations.shape[0]
    devices = lax.axis_size("seq")
    parts = lax.axis_size("tp")
    block_len = local_rows * devices // owners.shape[0]
    blocks_dev = owners.shape[0] // devices
    few = devices <= 8 and 1 < parts <= 8 and is_power(devices) and is_power(parts)
    if not few or block_len % 16 or blocks_dev < 2:
        return gathered_device(activations, queries, key_weight, value_weight, lengths, owners)
    first = (blocks_dev // 2) * block_len
    sizes = [first, local_rows - first]
    return chunked_device(activations, queries, key_weight, value_weight, lengths, owners, sizes)


def solution(mesh):
    rows = P(("groups", "seq"), "tp")
    columns = P(None, "tp")

    return jax.shard_map(
        per_device,
        mesh=mesh,
        in_specs=(rows, rows, columns, columns, P("groups"), P("groups")),
        out_specs=(rows, P(("groups", "seq"), "tp", None)),
        check_vma=False,
    )
```

```python
import functools

import jax
import jax.numpy as jnp
import numpy as np
from jax import lax
from jax.experimental import pallas as pl
from jax.experimental.pallas import tpu as pltpu
from jax.sharding import PartitionSpec as P

HD = 128
LOW = -1e30
TOGETHER = 8
MIB = 1 << 20
VMEM = pl.BlockSpec(memory_space=pltpu.VMEM)
SMEM = pl.BlockSpec(memory_space=pltpu.SMEM)
ANY = pl.BlockSpec(memory_space=pltpu.HBM)


def locate(row_ids, lengths):
    prompt_ends = jnp.cumsum(lengths)
    prompt_starts = prompt_ends - lengths
    segment = jnp.sum((row_ids[:, None] >= prompt_ends[None, :]).astype(jnp.int32), axis=1)
    numbers = jnp.arange(lengths.shape[0], dtype=jnp.int32)
    prompt_first = jnp.sum(
        jnp.where(segment[:, None] == numbers[None, :], prompt_starts[None, :], 0), axis=1
    )
    return (segment, row_ids - prompt_first)


def rotate(vectors, positions):
    half_size = vectors.shape[-1] // 2
    exponent = jnp.arange(half_size, dtype=jnp.float32) * (2.0 / vectors.shape[-1])
    inverse = jnp.exp(-exponent * jnp.log(jnp.float32(500000.0)))
    angles = positions.astype(jnp.float32)[:, None] * inverse[None, :]
    cosines = jnp.cos(angles)[:, None, :]
    sine_values = jnp.sin(angles)[:, None, :]
    lower_half = vectors[..., :half_size]
    upper_half = vectors[..., half_size:]
    return jnp.concatenate(
        [
            lower_half * cosines - upper_half * sine_values,
            upper_half * cosines + lower_half * sine_values,
        ],
        axis=-1,
    )


def swap(array, axis, distance):
    count = lax.axis_size(axis)
    return lax.ppermute(array, axis, [(i, i ^ distance) for i in range(count)])


def is_power(count):
    return count & (count - 1) == 0


def call(body, out_shape, in_specs, vmem=8 * MIB, scratch=(), out_specs=None):
    multiple = isinstance(out_shape, (list, tuple))
    return pl.pallas_call(
        body,
        out_shape=out_shape,
        in_specs=in_specs,
        out_specs=out_specs or ([VMEM] * len(out_shape) if multiple else VMEM),
        scratch_shapes=list(scratch),
        compiler_params=pltpu.CompilerParams(vmem_limit_bytes=vmem),
    )


def first_rows(rows, lengths_ref):
    first = jnp.zeros_like(rows)
    start = jnp.int32(0)
    for p in range(lengths_ref.shape[0]):
        first = jnp.where(rows >= start, start, first)
        start = start + lengths_ref[p]
    return first


def turn(vectors, cosines, sines):
    return vectors * cosines + pltpu.roll(vectors, HD // 2, 1) * sines


def prepare_body(place_ref, lengths_ref, inverse_ref, queries_ref, cos_ref, sin_ref, rotated_ref):
    local_rows, width = queries_ref.shape
    rows = place_ref[0] * local_rows + lax.broadcasted_iota(jnp.int32, (local_rows, HD), 0)
    positions = rows - first_rows(rows, lengths_ref)
    angles = positions.astype(jnp.float32) * inverse_ref[...]
    lanes = lax.broadcasted_iota(jnp.int32, (local_rows, HD), 1)
    cosines = jnp.cos(angles)
    sines = jnp.sin(angles)
    sines = jnp.where(lanes < HD // 2, -sines, sines)
    cos_ref[...] = cosines
    sin_ref[...] = sines
    for h in range(width // HD):
        vectors = queries_ref[:, h * HD : (h + 1) * HD].astype(jnp.float32)
        rotated_ref[:, h * HD : (h + 1) * HD] = turn(vectors, cosines, sines).astype(jnp.bfloat16)


def gathered_device(activations, queries, key_weight, value_weight, lengths, owners):
    local_rows = activations.shape[0]
    devices = lax.axis_size("seq")
    own_index = lax.axis_index("seq")
    kv_width = key_weight.shape[1]
    kv_heads = kv_width // HD
    query_heads = queries.shape[1] // HD
    group_size = query_heads // kv_heads
    row_ids = own_index * local_rows + jnp.arange(local_rows, dtype=jnp.int32)
    segment, positions = locate(row_ids, lengths)
    portion = lax.all_gather(activations, "tp", axis=1, tiled=True)
    key_rows = key_weight
    key_sums = jnp.dot(portion, key_rows, preferred_element_type=jnp.float32)
    value_sums = jnp.dot(portion, value_weight, preferred_element_type=jnp.float32)
    keys_local = rotate(key_sums.reshape(local_rows, kv_heads, HD), positions).astype(jnp.bfloat16)
    values_local = value_sums.astype(jnp.bfloat16).reshape(local_rows, kv_heads, HD)
    packed = jnp.concatenate([keys_local, values_local], axis=-1).reshape(
        local_rows, kv_heads * 2 * HD
    )
    rotated = rotate(queries.astype(jnp.float32).reshape(local_rows, query_heads, HD), positions)
    rotated = rotated.astype(jnp.bfloat16).reshape(local_rows, kv_heads, group_size, HD)

    def attend_block(running, portion, offset):
        running_max, running_sum, running_out = running
        amount = portion.shape[0]
        paired = portion.reshape(amount, kv_heads, 2 * HD)
        key_part = paired[:, :, :HD]
        value_part = paired[:, :, HD:]
        key_rows = offset + jnp.arange(amount, dtype=jnp.int32)
        key_segment, _ = locate(key_rows, lengths)
        allowed = (
            (key_segment[None, :] == segment[:, None])
            & (key_rows[None, :] <= row_ids[:, None])
            & (key_rows[None, :] >= 0)
        )
        allowed = allowed[:, None, None, :]
        scores = jnp.einsum(
            "qhgd,khd->qhgk", rotated, key_part, preferred_element_type=jnp.float32
        ) / jnp.sqrt(jnp.float32(HD))
        new_max = jnp.maximum(running_max, jnp.max(jnp.where(allowed, scores, -1e30), axis=-1))
        weights = jnp.where(allowed, jnp.exp(scores - new_max[..., None]), 0.0)
        factor = jnp.exp(running_max - new_max)
        running_sum = running_sum * factor + jnp.sum(weights, axis=-1)
        running_out = running_out * factor[..., None] + jnp.einsum(
            "qhgk,khd->qhgd",
            weights.astype(jnp.bfloat16),
            value_part,
            preferred_element_type=jnp.float32,
        )
        return (new_max, running_sum, running_out)

    def attend(running, portion, offset):
        amount = portion.shape[0]
        if amount > 512 and amount % 512 == 0:

            def advance(carried, entry):
                sub_portion, sub_offset = entry
                return (attend_block(carried, sub_portion, offset + sub_offset), None)

            offsets = jnp.arange(amount // 512, dtype=jnp.int32) * 512
            running, _ = lax.scan(
                advance, running, (portion.reshape(amount // 512, 512, portion.shape[1]), offsets)
            )
            return running
        return attend_block(running, portion, offset)

    initial = (
        jnp.full((local_rows, kv_heads, group_size), -1e30, jnp.float32),
        jnp.zeros((local_rows, kv_heads, group_size), jnp.float32),
        jnp.zeros((local_rows, kv_heads, group_size, HD), jnp.float32),
    )
    blocks_dev = owners.shape[0] // devices
    block_len = local_rows // blocks_dev
    is_own = owners == own_index
    ordinal = jnp.cumsum(is_own.astype(jnp.int32)) - 1
    matches = is_own[None, :] & (
        ordinal[None, :] == jnp.arange(blocks_dev, dtype=jnp.int32)[:, None]
    )
    leading = jnp.sum(
        jnp.where(matches, jnp.arange(owners.shape[0], dtype=jnp.int32)[None, :], 0), axis=1
    )
    within = jnp.arange(local_rows, dtype=jnp.int32)
    wanted = jnp.repeat(leading, block_len) * block_len + within % block_len
    portion = lax.all_gather(packed, "seq", axis=0, tiled=True)
    amount = portion.shape[0]
    choose = (wanted[:, None] == jnp.arange(amount, dtype=jnp.int32)[None, :]).astype(jnp.bfloat16)
    running = attend(
        (initial, jnp.zeros((local_rows, packed.shape[1]), jnp.float32))[0], portion, jnp.int32(0)
    )
    taken = jnp.dot(choose, portion, preferred_element_type=jnp.float32)
    kv_cache = taken.astype(jnp.bfloat16).reshape(local_rows, kv_heads, 2 * HD)
    _, running_sum, running_out = running
    attention = (
        (running_out / running_sum[..., None])
        .astype(jnp.bfloat16)
        .reshape(local_rows, query_heads * HD)
    )
    return (attention, kv_cache)


def add_products(piece, key_ref, value_ref, sums):
    kv_width = key_ref.shape[1]
    for at, ref in ((0, key_ref), (kv_width, value_ref)):
        sums[at] = sums[at] + jnp.dot(piece, ref[...], preferred_element_type=jnp.float32)


def early_body(offsets, place_ref, key_hbm, value_hbm, own_hbm, *refs):
    near_refs = refs[: len(offsets) - 1]
    keys_ref, values_ref, sums_ref, own_ref, weight_sems, own_sem = refs[len(offsets) - 1 :]
    parts, width, kv_width = keys_ref.shape
    copies = []
    own_copy = pltpu.make_async_copy(own_hbm, own_ref, own_sem)
    order = list(offsets) + [o for o in range(parts) if o not in offsets]
    for n, offset in enumerate(order):
        start = pl.multiple_of((place_ref[1] ^ offset) * width, width)
        pair = [
            pltpu.make_async_copy(hbm.at[pl.ds(start, width)], ref.at[offset], weight_sems.at[side, offset])
            for side, (hbm, ref) in enumerate(((key_hbm, keys_ref), (value_hbm, values_ref)))
        ]
        for copy in pair:
            copy.start()
        copies.append(pair)
        if n == 0:
            own_copy.start()
    own_copy.wait()
    sums = {0: 0.0, kv_width: 0.0}
    pieces = [own_ref] + list(near_refs)
    for n, offset in enumerate(order):
        for copy in copies[n]:
            copy.wait()
        if n < len(offsets):
            add_products(pieces[n][...], keys_ref.at[offset], values_ref.at[offset], sums)
    for at in sums:
        sums_ref[:, at : at + kv_width] = sums[at]


def far_body(offset, start, keys_ref, values_ref, sums_ref, piece_ref, out_ref):
    size = piece_ref.shape[0]
    kv_width = keys_ref.shape[2]
    rows = slice(start, start + size)
    sums = {at: sums_ref[rows, at : at + kv_width] for at in (0, kv_width)}
    add_products(piece_ref[...], keys_ref.at[offset], values_ref.at[offset], sums)
    for at in sums:
        out_ref[:, at : at + kv_width] = sums[at]


def late_body(offsets, start, keys_ref, values_ref, sums_ref, cos_ref, sin_ref, *refs):
    packed_ref = refs[-1]
    size = packed_ref.shape[0]
    kv_width = keys_ref.shape[2]
    rows = slice(start, start + size)
    sums = {at: sums_ref[:, at : at + kv_width] for at in (0, kv_width)}
    for offset, ref in zip(offsets, refs):
        add_products(ref[...], keys_ref.at[offset], values_ref.at[offset], sums)
    cosines = cos_ref[rows, :]
    sines = sin_ref[rows, :]
    for h in range(kv_width // HD):
        part = slice(h * HD, (h + 1) * HD)
        base = 2 * h * HD
        packed_ref[:, base : base + HD] = turn(sums[0][:, part], cosines, sines).astype(jnp.bfloat16)
        packed_ref[:, base + HD : base + 2 * HD] = sums[kv_width][:, part].astype(jnp.bfloat16)


def widen(column, amount):
    count = -(-amount // HD)
    wide = jnp.concatenate([column] * count, axis=1) if count > 1 else column
    return wide[:, :amount]


def attend_body(held, starts, carried, final, devices, place_ref, lengths_ref, owners_ref, rotated_ref, *refs):
    local_rows, width = rotated_ref.shape
    own = place_ref[0]
    count = devices * len(starts) if final else len(held)
    blocks = refs[:count]
    rest = refs[count:]
    old = rest[:3] if carried else ()
    rest = rest[len(old) :]
    parts = [blocks[c * devices + k] for k, c in held] if final else blocks
    amount = sum(ref.shape[0] for ref in parts)
    columns = lax.broadcasted_iota(jnp.int32, (local_rows, amount), 1)
    rows = own * local_rows + lax.broadcasted_iota(jnp.int32, (local_rows, amount), 0)
    key_rows = columns
    at = 0
    for (k, c), ref in zip(held, parts):
        moved = columns + ((own ^ k) * local_rows + (starts[c] - at))
        key_rows = jnp.where(columns >= at, moved, key_rows) if at else moved
        at += ref.shape[0]
    allowed = (key_rows >= first_rows(rows, lengths_ref)) & (key_rows <= rows)
    scale = float(HD) ** -0.5
    kv_heads = parts[0].shape[1] // (2 * HD)
    query_heads = width // HD
    group_size = query_heads // kv_heads
    for j in range(kv_heads):
        base = 2 * j * HD
        keys = jnp.concatenate([ref[:, base : base + HD] for ref in parts], axis=0)
        values = jnp.concatenate([ref[:, base + HD : base + 2 * HD] for ref in parts], axis=0)
        heads = range(j * group_size, (j + 1) * group_size)
        for at in range(0, group_size, TOGETHER):
            some = [slice(h * HD, (h + 1) * HD) for h in heads[at : at + TOGETHER]]
            scores = [
                lax.dot_general(
                    rotated_ref[:, lanes],
                    keys,
                    (((1,), (1,)), ((), ())),
                    preferred_element_type=jnp.float32,
                )
                for lanes in some
            ]
            olds = [[ref[:, lanes] for ref in old] for lanes in some]
            scores = [jnp.where(allowed, score, LOW) for score in scores]
            tops = [
                jnp.broadcast_to(jnp.max(score, axis=1, keepdims=True), (local_rows, HD))
                for score in scores
            ]
            if carried:
                tops = [jnp.maximum(top, past[0]) for top, past in zip(tops, olds)]
            weights = [
                jnp.exp((score - widen(top, amount)) * scale) for score, top in zip(scores, tops)
            ]
            totals = [
                jnp.broadcast_to(jnp.sum(weight, axis=1, keepdims=True), (local_rows, HD))
                for weight in weights
            ]
            outs = [
                jnp.dot(weight.astype(jnp.bfloat16), values, preferred_element_type=jnp.float32)
                for weight in weights
            ]
            if carried:
                factors = [jnp.exp((past[0] - top) * scale) for top, past in zip(tops, olds)]
                totals = [t + past[1] * f for t, past, f in zip(totals, olds, factors)]
                outs = [out + past[2] * f for out, past, f in zip(outs, olds, factors)]
            if final:
                for lanes, total, out in zip(some, totals, outs):
                    rest[0][:, lanes] = (out * (1.0 / total)).astype(jnp.bfloat16)
            else:
                for lanes, top, total, out in zip(some, tops, totals, outs):
                    rest[0][:, lanes] = top
                    rest[1][:, lanes] = total
                    rest[2][:, lanes] = out
    if final:
        fill_cache(blocks, starts, own, devices, local_rows, owners_ref, *rest[1:])


def fill_cache(blocks, starts, own, devices, local_rows, owners_ref, cache_ref, leading_ref):
    total_blocks = owners_ref.shape[0]
    blocks_dev = total_blocks // devices
    block_len = local_rows // blocks_dev
    count = jnp.int32(0)
    for b in range(total_blocks):
        hit = owners_ref[b] == own

        @pl.when(hit)
        def _(b=b, count=count):
            leading_ref[count] = b

        count = count + hit.astype(jnp.int32)
    for r in range(blocks_dev):
        block = leading_ref[r]
        distance = (block // blocks_dev) ^ own
        row = (block % blocks_dev) * block_len
        for c, start in enumerate(starts):
            for k in range(devices):
                ref = blocks[c * devices + k]
                inside = (distance == k) & (row >= start) & (row < start + ref.shape[0])

                @pl.when(inside)
                def _(ref=ref, start=start, row=row, r=r):
                    source = pl.ds(pl.multiple_of(row - start, block_len), block_len)
                    cache_ref[r * block_len : (r + 1) * block_len, :] = ref[source, :]


def chunked_device(activations, queries, key_weight, value_weight, lengths, owners, sizes):
    local_rows, width = activations.shape
    devices = lax.axis_size("seq")
    parts = lax.axis_size("tp")
    kv_width = key_weight.shape[1]
    place = jnp.stack([lax.axis_index("seq"), lax.axis_index("tp")]).astype(jnp.int32)
    starts = [sum(sizes[:c]) for c in range(len(sizes))]
    far = parts // 2

    def spread_over(pieces, distance):
        while distance:
            for offset in list(pieces):
                pieces[offset ^ distance] = swap(pieces[offset], "tp", distance)
            distance //= 2
        return pieces

    crossed = []
    for start, size in zip(starts, sizes):
        crossed.append(swap(activations[start : start + size], "tp", far))
    near = spread_over({0: activations}, far // 2)

    exponent = np.arange(HD // 2) * (2.0 / HD)
    inverse = np.exp(-exponent * np.log(500000.0)).astype(np.float32)
    inverse = jnp.asarray(np.concatenate([inverse, inverse])[None, :])
    table = jax.ShapeDtypeStruct((local_rows, HD), jnp.float32)
    cosines, sines, rotated = call(
        prepare_body,
        [table, table, jax.ShapeDtypeStruct(queries.shape, jnp.bfloat16)],
        [SMEM, SMEM, VMEM, VMEM],
    )(place, lengths, inverse, queries)
    offsets = sorted(near)
    stays = [pltpu.with_memory_space_constraint(a, pltpu.HBM) for a in (key_weight, value_weight, activations)]
    weights = jax.ShapeDtypeStruct((parts, width, kv_width), jnp.bfloat16)
    keys, values, sums = call(
        functools.partial(early_body, offsets),
        [weights, weights, jax.ShapeDtypeStruct((local_rows, 2 * kv_width), jnp.float32)],
        [SMEM] + [ANY] * 3 + [VMEM] * (len(offsets) - 1),
        scratch=[
            pltpu.VMEM(activations.shape, activations.dtype),
            pltpu.SemaphoreType.DMA((2, parts)),
            pltpu.SemaphoreType.DMA,
        ],
    )(place, *stays, *[near[o] for o in offsets[1:]])

    arrived = []
    ready = sums
    for piece, start, size in zip(crossed, starts, sizes):
        piece = lax.optimization_barrier((piece, ready))[0]
        late = spread_over({far: piece}, far // 2)
        del late[far]
        partial = call(
            functools.partial(far_body, far, start),
            jax.ShapeDtypeStruct((size, 2 * kv_width), jnp.float32),
            [VMEM] * 4,
        )(keys, values, sums, piece)
        offsets = sorted(late)
        packed = call(
            functools.partial(late_body, offsets, start),
            jax.ShapeDtypeStruct((size, 2 * kv_width), jnp.bfloat16),
            [VMEM] * (5 + len(offsets)),
        )(keys, values, partial, cosines, sines, *[late[o] for o in offsets])
        ready = packed
        blocks = [packed]
        for k in range(1, devices):
            blocks.append(swap(packed, "seq", k))
        arrived.append(blocks)

    last = len(sizes) - 1
    half = devices // 2
    stages = [[(k, c) for k in range(devices)] for c in range(last)]
    if half:
        stages.append([(k, last) for k in range(half)])
    stages.append([(k, last) for k in range(half, devices)])
    state = ()
    for n, held in enumerate(stages):
        final = n == len(stages) - 1
        if final:
            taken = [block for blocks in arrived for block in blocks]
            results = [
                jax.ShapeDtypeStruct(queries.shape, jnp.bfloat16),
                jax.ShapeDtypeStruct((local_rows, 2 * kv_width), jnp.bfloat16),
            ]
        else:
            taken = [arrived[c][k] for k, c in held]
            results = [jax.ShapeDtypeStruct(queries.shape, jnp.float32)] * 3
        state = call(
            functools.partial(attend_body, held, starts, n > 0, final, devices),
            results,
            [SMEM] * 3 + [VMEM] * (1 + len(taken) + len(state)),
            scratch=[pltpu.SMEM((owners.shape[0] // devices,), jnp.int32)] if final else (),
        )(place, lengths, owners, rotated, *taken, *state)
    attention, cache = state
    return attention, cache.reshape(local_rows, kv_width // HD, 2 * HD)


def chunk_sizes(local_rows, block_len):
    first = (local_rows // block_len // 2) * block_len
    return [first, local_rows - first]


def per_device(activations, queries, key_weight, value_weight, lengths, owners):
    local_rows = activations.shape[0]
    devices = lax.axis_size("seq")
    parts = lax.axis_size("tp")
    blocks_dev = owners.shape[0] // devices
    block_len = local_rows // blocks_dev
    few = devices <= 8 and 1 < parts <= 8 and is_power(devices) and is_power(parts)
    if not few or block_len % 16 or blocks_dev < 2:
        return gathered_device(activations, queries, key_weight, value_weight, lengths, owners)
    sizes = chunk_sizes(local_rows, block_len)
    return chunked_device(activations, queries, key_weight, value_weight, lengths, owners, sizes)


def solution(mesh):
    rows = P(("groups", "seq"), "tp")
    columns = P(None, "tp")

    return jax.shard_map(
        per_device,
        mesh=mesh,
        in_specs=(rows, rows, columns, columns, P("groups"), P("groups")),
        out_specs=(rows, P(("groups", "seq"), "tp", None)),
        check_vma=False,
    )
```

```python
import functools

import jax
import jax.numpy as jnp
import numpy as np
from jax import lax
from jax.experimental import pallas as pl
from jax.experimental.pallas import tpu as pltpu
from jax.sharding import PartitionSpec as P

HD = 128
LOW = -1e30
TOGETHER = 16
MIB = 1 << 20
VMEM = pl.BlockSpec(memory_space=pltpu.VMEM)
SMEM = pl.BlockSpec(memory_space=pltpu.SMEM)
ANY = pl.BlockSpec(memory_space=pltpu.HBM)


def locate(row_ids, lengths):
    prompt_ends = jnp.cumsum(lengths)
    prompt_starts = prompt_ends - lengths
    segment = jnp.sum((row_ids[:, None] >= prompt_ends[None, :]).astype(jnp.int32), axis=1)
    numbers = jnp.arange(lengths.shape[0], dtype=jnp.int32)
    prompt_first = jnp.sum(
        jnp.where(segment[:, None] == numbers[None, :], prompt_starts[None, :], 0), axis=1
    )
    return (segment, row_ids - prompt_first)


def rotate(vectors, positions):
    half_size = vectors.shape[-1] // 2
    exponent = jnp.arange(half_size, dtype=jnp.float32) * (2.0 / vectors.shape[-1])
    inverse = jnp.exp(-exponent * jnp.log(jnp.float32(500000.0)))
    angles = positions.astype(jnp.float32)[:, None] * inverse[None, :]
    cosines = jnp.cos(angles)[:, None, :]
    sine_values = jnp.sin(angles)[:, None, :]
    lower_half = vectors[..., :half_size]
    upper_half = vectors[..., half_size:]
    return jnp.concatenate(
        [
            lower_half * cosines - upper_half * sine_values,
            upper_half * cosines + lower_half * sine_values,
        ],
        axis=-1,
    )


def swap(array, axis, distance):
    count = lax.axis_size(axis)
    return lax.ppermute(array, axis, [(i, i ^ distance) for i in range(count)])


def is_power(count):
    return count & (count - 1) == 0


def call(body, out_shape, in_specs, vmem=8 * MIB, scratch=(), out_specs=None, aliases={}):
    multiple = isinstance(out_shape, (list, tuple))
    return pl.pallas_call(
        body,
        out_shape=out_shape,
        in_specs=in_specs,
        out_specs=out_specs or ([VMEM] * len(out_shape) if multiple else VMEM),
        scratch_shapes=list(scratch),
        input_output_aliases=aliases,
        compiler_params=pltpu.CompilerParams(vmem_limit_bytes=vmem),
    )


def first_rows(rows, lengths_ref):
    first = jnp.zeros_like(rows)
    start = jnp.int32(0)
    for p in range(lengths_ref.shape[0]):
        first = jnp.where(rows >= start, start, first)
        start = start + lengths_ref[p]
    return first


def turn(vectors, cosines, sines):
    return vectors * cosines + pltpu.roll(vectors, HD // 2, 1) * sines


def gathered_device(activations, queries, key_weight, value_weight, lengths, owners):
    local_rows = activations.shape[0]
    devices = lax.axis_size("seq")
    own_index = lax.axis_index("seq")
    kv_width = key_weight.shape[1]
    kv_heads = kv_width // HD
    query_heads = queries.shape[1] // HD
    group_size = query_heads // kv_heads
    row_ids = own_index * local_rows + jnp.arange(local_rows, dtype=jnp.int32)
    segment, positions = locate(row_ids, lengths)
    portion = lax.all_gather(activations, "tp", axis=1, tiled=True)
    key_rows = key_weight
    key_sums = jnp.dot(portion, key_rows, preferred_element_type=jnp.float32)
    value_sums = jnp.dot(portion, value_weight, preferred_element_type=jnp.float32)
    keys_local = rotate(key_sums.reshape(local_rows, kv_heads, HD), positions).astype(jnp.bfloat16)
    values_local = value_sums.astype(jnp.bfloat16).reshape(local_rows, kv_heads, HD)
    packed = jnp.concatenate([keys_local, values_local], axis=-1).reshape(
        local_rows, kv_heads * 2 * HD
    )
    rotated = rotate(queries.astype(jnp.float32).reshape(local_rows, query_heads, HD), positions)
    rotated = rotated.astype(jnp.bfloat16).reshape(local_rows, kv_heads, group_size, HD)

    def attend_block(running, portion, offset):
        running_max, running_sum, running_out = running
        amount = portion.shape[0]
        paired = portion.reshape(amount, kv_heads, 2 * HD)
        key_part = paired[:, :, :HD]
        value_part = paired[:, :, HD:]
        key_rows = offset + jnp.arange(amount, dtype=jnp.int32)
        key_segment, _ = locate(key_rows, lengths)
        allowed = (
            (key_segment[None, :] == segment[:, None])
            & (key_rows[None, :] <= row_ids[:, None])
            & (key_rows[None, :] >= 0)
        )
        allowed = allowed[:, None, None, :]
        scores = jnp.einsum(
            "qhgd,khd->qhgk", rotated, key_part, preferred_element_type=jnp.float32
        ) / jnp.sqrt(jnp.float32(HD))
        new_max = jnp.maximum(running_max, jnp.max(jnp.where(allowed, scores, -1e30), axis=-1))
        weights = jnp.where(allowed, jnp.exp(scores - new_max[..., None]), 0.0)
        factor = jnp.exp(running_max - new_max)
        running_sum = running_sum * factor + jnp.sum(weights, axis=-1)
        running_out = running_out * factor[..., None] + jnp.einsum(
            "qhgk,khd->qhgd",
            weights.astype(jnp.bfloat16),
            value_part,
            preferred_element_type=jnp.float32,
        )
        return (new_max, running_sum, running_out)

    def attend(running, portion, offset):
        amount = portion.shape[0]
        if amount > 512 and amount % 512 == 0:

            def advance(carried, entry):
                sub_portion, sub_offset = entry
                return (attend_block(carried, sub_portion, offset + sub_offset), None)

            offsets = jnp.arange(amount // 512, dtype=jnp.int32) * 512
            running, _ = lax.scan(
                advance, running, (portion.reshape(amount // 512, 512, portion.shape[1]), offsets)
            )
            return running
        return attend_block(running, portion, offset)

    initial = (
        jnp.full((local_rows, kv_heads, group_size), -1e30, jnp.float32),
        jnp.zeros((local_rows, kv_heads, group_size), jnp.float32),
        jnp.zeros((local_rows, kv_heads, group_size, HD), jnp.float32),
    )
    blocks_dev = owners.shape[0] // devices
    block_len = local_rows // blocks_dev
    is_own = owners == own_index
    ordinal = jnp.cumsum(is_own.astype(jnp.int32)) - 1
    matches = is_own[None, :] & (
        ordinal[None, :] == jnp.arange(blocks_dev, dtype=jnp.int32)[:, None]
    )
    leading = jnp.sum(
        jnp.where(matches, jnp.arange(owners.shape[0], dtype=jnp.int32)[None, :], 0), axis=1
    )
    within = jnp.arange(local_rows, dtype=jnp.int32)
    wanted = jnp.repeat(leading, block_len) * block_len + within % block_len
    portion = lax.all_gather(packed, "seq", axis=0, tiled=True)
    amount = portion.shape[0]
    choose = (wanted[:, None] == jnp.arange(amount, dtype=jnp.int32)[None, :]).astype(jnp.bfloat16)
    running = attend(
        (initial, jnp.zeros((local_rows, packed.shape[1]), jnp.float32))[0], portion, jnp.int32(0)
    )
    taken = jnp.dot(choose, portion, preferred_element_type=jnp.float32)
    kv_cache = taken.astype(jnp.bfloat16).reshape(local_rows, kv_heads, 2 * HD)
    _, running_sum, running_out = running
    attention = (
        (running_out / running_sum[..., None])
        .astype(jnp.bfloat16)
        .reshape(local_rows, query_heads * HD)
    )
    return (attention, kv_cache)


def prepare(own, lengths_ref, owners_ref, queries_ref, cos_ref, sin_ref, rotated_ref, facts_ref, slots_ref):
    local_rows, width = queries_ref.shape
    rows = own * local_rows + lax.broadcasted_iota(jnp.int32, (local_rows, HD), 0)
    positions = rows - first_rows(rows, lengths_ref)
    half = HD // 2
    lanes = lax.broadcasted_iota(jnp.int32, (local_rows, HD), 1)
    exponent = jnp.where(lanes < half, lanes, lanes - half).astype(jnp.float32) * (2.0 / HD)
    inverse = jnp.exp(-exponent * jnp.log(jnp.float32(500000.0)))
    angles = positions.astype(jnp.float32) * inverse
    cosines = jnp.cos(angles)
    sines = jnp.sin(angles)
    sines = jnp.where(lanes < half, -sines, sines)
    cos_ref[...] = cosines
    sin_ref[...] = sines
    for h in range(width // HD):
        vectors = queries_ref[:, h * HD : (h + 1) * HD].astype(jnp.float32)
        rotated_ref[:, h * HD : (h + 1) * HD] = turn(vectors, cosines, sines).astype(jnp.bfloat16)
    rows = own * local_rows + lax.broadcasted_iota(jnp.int32, (1, local_rows), 1)
    facts_ref[0:1, :] = first_rows(rows, lengths_ref)
    facts_ref[1:2, :] = rows
    facts_ref[2:3, :] = jnp.zeros_like(rows) + own
    count = jnp.int32(0)
    for b in range(owners_ref.shape[0]):
        hit = owners_ref[b] == own
        slots_ref[b] = jnp.where(hit, count, -1)
        count = count + hit.astype(jnp.int32)
    slots_ref[owners_ref.shape[0]] = own


def add_products(piece, key_ref, value_ref, sums):
    kv_width = key_ref.shape[1]
    for at, ref in ((0, key_ref), (kv_width, value_ref)):
        sums[at] = sums[at] + jnp.dot(piece, ref[...], preferred_element_type=jnp.float32)


def early_body(offsets, place_ref, key_hbm, value_hbm, own_hbm, queries_hbm, lengths_hbm, owners_hbm, *refs):
    near_refs = refs[: len(offsets) - 1]
    outs = refs[len(offsets) - 1 :]
    keys_ref, values_ref, sums_ref = outs[:3]
    tables = outs[3:8]
    own_ref, queries_ref, lengths_ref, owners_ref, weight_sems, sems = outs[8:]
    parts, width, kv_width = keys_ref.shape
    small = [
        pltpu.make_async_copy(source, goal, sems.at[n])
        for n, (source, goal) in enumerate(
            (
                (lengths_hbm, lengths_ref),
                (owners_hbm, owners_ref),
                (queries_hbm, queries_ref),
                (own_hbm, own_ref),
            )
        )
    ]
    for copy in small:
        copy.start()
    copies = []
    order = list(offsets) + [o for o in range(parts) if o not in offsets]
    for offset in order:
        start = pl.multiple_of((place_ref[1] ^ offset) * width, width)
        pair = [
            pltpu.make_async_copy(hbm.at[pl.ds(start, width)], ref.at[offset], weight_sems.at[side, offset])
            for side, (hbm, ref) in enumerate(((key_hbm, keys_ref), (value_hbm, values_ref)))
        ]
        for copy in pair:
            copy.start()
        copies.append(pair)
    for copy in small:
        copy.wait()
    prepare(place_ref[0], lengths_ref, owners_ref, queries_ref, *tables)
    sums = {0: 0.0, kv_width: 0.0}
    pieces = [own_ref] + list(near_refs)
    for n, offset in enumerate(order):
        for copy in copies[n]:
            copy.wait()
        if n < len(offsets):
            add_products(pieces[n][...], keys_ref.at[offset], values_ref.at[offset], sums)
    for at in sums:
        sums_ref[:, at : at + kv_width] = sums[at]


def far_body(offset, start, keys_ref, values_ref, sums_ref, piece_ref, out_ref):
    size = piece_ref.shape[0]
    kv_width = keys_ref.shape[2]
    rows = slice(start, start + size)
    sums = {at: sums_ref[rows, at : at + kv_width] for at in (0, kv_width)}
    add_products(piece_ref[...], keys_ref.at[offset], values_ref.at[offset], sums)
    for at in sums:
        out_ref[:, at : at + kv_width] = sums[at]


def late_body(offsets, start, keys_ref, values_ref, sums_ref, cos_ref, sin_ref, *refs):
    packed_ref = refs[-1]
    size = packed_ref.shape[0]
    kv_width = keys_ref.shape[2]
    rows = slice(start, start + size)
    sums = {at: sums_ref[:, at : at + kv_width] for at in (0, kv_width)}
    for offset, ref in zip(offsets, refs):
        add_products(ref[...], keys_ref.at[offset], values_ref.at[offset], sums)
    cosines = cos_ref[rows, :]
    sines = sin_ref[rows, :]
    for h in range(kv_width // HD):
        part = slice(h * HD, (h + 1) * HD)
        base = 2 * h * HD
        packed_ref[:, base : base + HD] = turn(sums[0][:, part], cosines, sines).astype(jnp.bfloat16)
        packed_ref[:, base + HD : base + 2 * HD] = sums[kv_width][:, part].astype(jnp.bfloat16)


def attend_body(held, spans, carried, final, facts_ref, slots_hbm, rotated_ref, *refs):
    local_rows, width = rotated_ref.shape
    starts, block_len = spans
    parts = refs[: len(held)]
    rest = refs[len(held) :]
    old = rest[:4] if carried else ()
    rest = rest[len(old) :]
    slots_ref, slots_sem = rest[-2:]
    cache_ref = rest[-3]
    fetch = pltpu.make_async_copy(slots_hbm, slots_ref, slots_sem)
    fetch.start()
    amount = sum(ref.shape[0] for ref in parts)
    order = lax.broadcasted_iota(jnp.int32, (amount, local_rows), 0)
    own = facts_ref[2:3, :]
    key_rows = order
    at = 0
    for (k, c), ref in zip(held, parts):
        moved = order + ((own ^ k) * local_rows + (starts[c] - at))
        key_rows = jnp.where(order >= at, moved, key_rows) if at else moved
        at += ref.shape[0]
    allowed = (key_rows >= facts_ref[0:1, :]) & (key_rows <= facts_ref[1:2, :])
    scale = float(HD**-0.5 * np.log2(np.e))
    kv_heads = parts[0].shape[1] // (2 * HD)
    query_heads = width // HD
    group_size = query_heads // kv_heads
    if final:
        lines = lax.broadcasted_iota(jnp.int32, (local_rows, local_rows), 0)
        lanes = lax.broadcasted_iota(jnp.int32, (local_rows, local_rows), 1)
        identity = (lines == lanes).astype(jnp.bfloat16)
    keys = []
    values = []
    for j in range(kv_heads):
        base = 2 * j * HD
        keys.append(jnp.concatenate([ref[:, base : base + HD] for ref in parts], axis=0))
        value = jnp.concatenate([ref[:, base + HD : base + 2 * HD] for ref in parts], axis=0)
        values.append(value.T)
    for at in range(0, query_heads, TOGETHER):
        some = range(query_heads)[at : at + TOGETHER]
        parts_of = [slice(h * HD, (h + 1) * HD) for h in some]
        scores = [
            lax.dot_general(
                keys[h // group_size],
                rotated_ref[:, part],
                (((1,), (1,)), ((), ())),
                preferred_element_type=jnp.float32,
            )
            for h, part in zip(some, parts_of)
        ]
        if carried:
            old_tops = [old[0][h : h + 1, :] for h in some]
            old_totals = [old[1][h : h + 1, :] for h in some]
            old_outs = [old[2][part, :] for part in parts_of]
        scores = [jnp.where(allowed, score, LOW) for score in scores]
        tops = [jnp.max(score, axis=0, keepdims=True) for score in scores]
        if carried:
            tops = [jnp.maximum(top, past) for top, past in zip(tops, old_tops)]
        weights = [jnp.exp2((score - top) * scale) for score, top in zip(scores, tops)]
        totals = [jnp.sum(weight, axis=0, keepdims=True) for weight in weights]
        outs = [
            jnp.dot(
                values[h // group_size],
                weight.astype(jnp.bfloat16),
                preferred_element_type=jnp.float32,
            )
            for h, weight in zip(some, weights)
        ]
        if carried:
            factors = [jnp.exp2((past - top) * scale) for top, past in zip(tops, old_tops)]
            totals = [t + past * f for t, past, f in zip(totals, old_totals, factors)]
            outs = [out + past * f for out, past, f in zip(outs, old_outs, factors)]
        if final:
            outs = [(out * (1.0 / total)).astype(jnp.bfloat16) for out, total in zip(outs, totals)]
            for part, out in zip(parts_of, outs):
                rest[0][:, part] = lax.dot_general(
                    identity,
                    out,
                    (((1,), (1,)), ((), ())),
                    preferred_element_type=jnp.float32,
                ).astype(jnp.bfloat16)
        else:
            for h, part, top, total, out in zip(some, parts_of, tops, totals, outs):
                rest[0][h : h + 1, :] = top
                rest[1][h : h + 1, :] = total
                rest[2][part, :] = out
    if carried:
        cache_ref[...] = old[3][...]
    fetch.wait()
    own = slots_ref[slots_ref.shape[0] - 1]
    blocks_dev = local_rows // block_len
    for (k, c), ref in zip(held, parts):
        at = 0
        while at < ref.shape[0]:
            row = starts[c] + at
            size = min(block_len - row % block_len, ref.shape[0] - at)
            slot = slots_ref[(own ^ k) * blocks_dev + row // block_len]

            @pl.when(slot >= 0)
            def _(ref=ref, at=at, row=row, size=size, slot=slot):
                goal = pl.multiple_of(slot * block_len + row % block_len, 16)
                block = ref[at : at + size, :]
                cache_ref[pl.ds(goal, size)] = block.reshape((size,) + cache_ref.shape[1:])

            at += size


def chunked_device(activations, queries, key_weight, value_weight, lengths, owners, sizes):
    local_rows, width = activations.shape
    devices = lax.axis_size("seq")
    parts = lax.axis_size("tp")
    kv_width = key_weight.shape[1]
    place = jnp.stack([lax.axis_index("seq"), lax.axis_index("tp")]).astype(jnp.int32)
    starts = [sum(sizes[:c]) for c in range(len(sizes))]
    far = parts // 2

    def spread_over(pieces, distance):
        while distance:
            for offset in list(pieces):
                pieces[offset ^ distance] = swap(pieces[offset], "tp", distance)
            distance //= 2
        return pieces

    crossed = []
    stays = [
        pltpu.with_memory_space_constraint(a, pltpu.HBM)
        for a in (key_weight, value_weight, activations, queries, lengths, owners)
    ]
    for start, size in zip(starts, sizes):
        piece = activations[start : start + size]
        crossed.append(swap(piece, "tp", far))
    near = spread_over({0: activations}, far // 2)

    offsets = sorted(near)
    table = jax.ShapeDtypeStruct((local_rows, HD), jnp.float32)
    weights = jax.ShapeDtypeStruct((parts, width, kv_width), jnp.bfloat16)
    keys, values, sums, cosines, sines, rotated, facts, slots = call(
        functools.partial(early_body, offsets),
        [
            weights,
            weights,
            jax.ShapeDtypeStruct((local_rows, 2 * kv_width), jnp.float32),
            table,
            table,
            jax.ShapeDtypeStruct(queries.shape, queries.dtype),
            jax.ShapeDtypeStruct((8, local_rows), jnp.int32),
            jax.ShapeDtypeStruct((owners.shape[0] + 1,), jnp.int32),
        ],
        [SMEM] + [ANY] * 6 + [VMEM] * (len(offsets) - 1),
        scratch=[
            pltpu.VMEM(activations.shape, activations.dtype),
            pltpu.VMEM(queries.shape, queries.dtype),
            pltpu.SMEM(lengths.shape, jnp.int32),
            pltpu.SMEM(owners.shape, jnp.int32),
            pltpu.SemaphoreType.DMA((2, parts)),
            pltpu.SemaphoreType.DMA((4,)),
        ],
        out_specs=[VMEM] * 7 + [SMEM],
    )(place, *stays, *[near[o] for o in offsets[1:]])

    arrived = []
    ready = sums
    for piece, start, size in zip(crossed, starts, sizes):
        piece = lax.optimization_barrier((piece, ready))[0]
        late = spread_over({far: piece}, far // 2)
        del late[far]
        partial = call(
            functools.partial(far_body, far, start),
            jax.ShapeDtypeStruct((size, 2 * kv_width), jnp.float32),
            [VMEM] * 4,
        )(keys, values, sums, piece)
        offsets = sorted(late)
        packed = call(
            functools.partial(late_body, offsets, start),
            jax.ShapeDtypeStruct((size, 2 * kv_width), jnp.bfloat16),
            [VMEM] * (5 + len(offsets)),
        )(keys, values, partial, cosines, sines, *[late[o] for o in offsets])
        ready = packed
        blocks = [packed]
        for k in range(1, devices):
            blocks.append(swap(packed, "seq", k))
        arrived.append(blocks)

    last = len(sizes) - 1
    half = devices // 2
    stages = [[(k, c) for k in range(devices)] for c in range(last)]
    if half:
        stages.append([(k, last) for k in range(half)])
    stages.append([(k, last) for k in range(half, devices)])
    state = ()
    spans = (starts, local_rows * devices // owners.shape[0])
    cache = jax.ShapeDtypeStruct((local_rows, kv_width // HD, 2 * HD), jnp.bfloat16)
    query_width = queries.shape[1]
    line = jax.ShapeDtypeStruct((query_width // HD, local_rows), jnp.float32)
    for n, held in enumerate(stages):
        final = n == len(stages) - 1
        taken = [arrived[c][k] for k, c in held]
        if final:
            results = [jax.ShapeDtypeStruct(queries.shape, jnp.bfloat16)]
        else:
            results = [line, line, jax.ShapeDtypeStruct((query_width, local_rows), jnp.float32)]
        state = call(
            functools.partial(attend_body, held, spans, n > 0, final),
            results + [cache],
            [VMEM, ANY] + [VMEM] * (1 + len(taken) + len(state)),
            scratch=[pltpu.SMEM(slots.shape, jnp.int32), pltpu.SemaphoreType.DMA],
        )(facts, slots, rotated, *taken, *state)
    return state


def chunk_sizes(local_rows, block_len):
    first = (local_rows // block_len // 2) * block_len
    return [first, local_rows - first]


def per_device(activations, queries, key_weight, value_weight, lengths, owners):
    local_rows = activations.shape[0]
    devices = lax.axis_size("seq")
    parts = lax.axis_size("tp")
    blocks_dev = owners.shape[0] // devices
    block_len = local_rows // blocks_dev
    few = devices <= 8 and 1 < parts <= 8 and is_power(devices) and is_power(parts)
    if not few or block_len % 16 or blocks_dev < 2:
        return gathered_device(activations, queries, key_weight, value_weight, lengths, owners)
    sizes = chunk_sizes(local_rows, block_len)
    return chunked_device(activations, queries, key_weight, value_weight, lengths, owners, sizes)


def solution(mesh):
    rows = P(("groups", "seq"), "tp")
    columns = P(None, "tp")

    return jax.shard_map(
        per_device,
        mesh=mesh,
        in_specs=(rows, rows, columns, columns, P("groups"), P("groups")),
        out_specs=(rows, P(("groups", "seq"), "tp", None)),
        check_vma=False,
    )
```

```python
import functools

import jax
import jax.numpy as jnp
import numpy as np
from jax import lax
from jax.experimental import pallas as pl
from jax.experimental.pallas import tpu as pltpu
from jax.sharding import PartitionSpec as P

HD = 128
LOW = -1e30
SHARE = 2
STAGES = ('acg', 'bf', 'd', 'e')
MIB = 1 << 20
VMEM = pl.BlockSpec(memory_space=pltpu.VMEM)
SMEM = pl.BlockSpec(memory_space=pltpu.SMEM)
ANY = pl.BlockSpec(memory_space=pltpu.HBM)


def locate(row_ids, lengths):
    prompt_ends = jnp.cumsum(lengths)
    prompt_starts = prompt_ends - lengths
    segment = jnp.sum((row_ids[:, None] >= prompt_ends[None, :]).astype(jnp.int32), axis=1)
    numbers = jnp.arange(lengths.shape[0], dtype=jnp.int32)
    prompt_first = jnp.sum(
        jnp.where(segment[:, None] == numbers[None, :], prompt_starts[None, :], 0), axis=1
    )
    return (segment, row_ids - prompt_first)


def rotate(vectors, positions):
    half_size = vectors.shape[-1] // 2
    exponent = jnp.arange(half_size, dtype=jnp.float32) * (2.0 / vectors.shape[-1])
    inverse = jnp.exp(-exponent * jnp.log(jnp.float32(500000.0)))
    angles = positions.astype(jnp.float32)[:, None] * inverse[None, :]
    cosines = jnp.cos(angles)[:, None, :]
    sine_values = jnp.sin(angles)[:, None, :]
    lower_half = vectors[..., :half_size]
    upper_half = vectors[..., half_size:]
    return jnp.concatenate(
        [
            lower_half * cosines - upper_half * sine_values,
            upper_half * cosines + lower_half * sine_values,
        ],
        axis=-1,
    )


def swap(array, axis, distance):
    count = lax.axis_size(axis)
    return lax.ppermute(array, axis, [(i, i ^ distance) for i in range(count)])


def is_power(count):
    return count & (count - 1) == 0


def call(body, out_shape, in_specs, vmem=8 * MIB, scratch=(), out_specs=None, aliases={}):
    multiple = isinstance(out_shape, (list, tuple))
    return pl.pallas_call(
        body,
        out_shape=out_shape,
        in_specs=in_specs,
        out_specs=out_specs or ([VMEM] * len(out_shape) if multiple else VMEM),
        scratch_shapes=list(scratch),
        input_output_aliases=aliases,
        compiler_params=pltpu.CompilerParams(vmem_limit_bytes=vmem),
    )


def first_rows(rows, lengths_ref):
    first = jnp.zeros_like(rows)
    start = jnp.int32(0)
    for p in range(lengths_ref.shape[0]):
        first = jnp.where(rows >= start, start, first)
        start = start + lengths_ref[p]
    return first


def turn(vectors, cosines, sines):
    return vectors * cosines + pltpu.roll(vectors, HD // 2, 1) * sines


def gathered_device(activations, queries, key_weight, value_weight, lengths, owners):
    local_rows = activations.shape[0]
    devices = lax.axis_size("seq")
    own_index = lax.axis_index("seq")
    kv_width = key_weight.shape[1]
    kv_heads = kv_width // HD
    query_heads = queries.shape[1] // HD
    group_size = query_heads // kv_heads
    row_ids = own_index * local_rows + jnp.arange(local_rows, dtype=jnp.int32)
    segment, positions = locate(row_ids, lengths)
    portion = lax.all_gather(activations, "tp", axis=1, tiled=True)
    key_rows = key_weight
    key_sums = jnp.dot(portion, key_rows, preferred_element_type=jnp.float32)
    value_sums = jnp.dot(portion, value_weight, preferred_element_type=jnp.float32)
    keys_local = rotate(key_sums.reshape(local_rows, kv_heads, HD), positions).astype(jnp.bfloat16)
    values_local = value_sums.astype(jnp.bfloat16).reshape(local_rows, kv_heads, HD)
    packed = jnp.concatenate([keys_local, values_local], axis=-1).reshape(
        local_rows, kv_heads * 2 * HD
    )
    rotated = rotate(queries.astype(jnp.float32).reshape(local_rows, query_heads, HD), positions)
    rotated = rotated.astype(jnp.bfloat16).reshape(local_rows, kv_heads, group_size, HD)

    def attend_block(running, portion, offset):
        running_max, running_sum, running_out = running
        amount = portion.shape[0]
        paired = portion.reshape(amount, kv_heads, 2 * HD)
        key_part = paired[:, :, :HD]
        value_part = paired[:, :, HD:]
        key_rows = offset + jnp.arange(amount, dtype=jnp.int32)
        key_segment, _ = locate(key_rows, lengths)
        allowed = (
            (key_segment[None, :] == segment[:, None])
            & (key_rows[None, :] <= row_ids[:, None])
            & (key_rows[None, :] >= 0)
        )
        allowed = allowed[:, None, None, :]
        scores = jnp.einsum(
            "qhgd,khd->qhgk", rotated, key_part, preferred_element_type=jnp.float32
        ) / jnp.sqrt(jnp.float32(HD))
        new_max = jnp.maximum(running_max, jnp.max(jnp.where(allowed, scores, -1e30), axis=-1))
        weights = jnp.where(allowed, jnp.exp(scores - new_max[..., None]), 0.0)
        factor = jnp.exp(running_max - new_max)
        running_sum = running_sum * factor + jnp.sum(weights, axis=-1)
        running_out = running_out * factor[..., None] + jnp.einsum(
            "qhgk,khd->qhgd",
            weights.astype(jnp.bfloat16),
            value_part,
            preferred_element_type=jnp.float32,
        )
        return (new_max, running_sum, running_out)

    def attend(running, portion, offset):
        amount = portion.shape[0]
        if amount > 512 and amount % 512 == 0:

            def advance(carried, entry):
                sub_portion, sub_offset = entry
                return (attend_block(carried, sub_portion, offset + sub_offset), None)

            offsets = jnp.arange(amount // 512, dtype=jnp.int32) * 512
            running, _ = lax.scan(
                advance, running, (portion.reshape(amount // 512, 512, portion.shape[1]), offsets)
            )
            return running
        return attend_block(running, portion, offset)

    initial = (
        jnp.full((local_rows, kv_heads, group_size), -1e30, jnp.float32),
        jnp.zeros((local_rows, kv_heads, group_size), jnp.float32),
        jnp.zeros((local_rows, kv_heads, group_size, HD), jnp.float32),
    )
    blocks_dev = owners.shape[0] // devices
    block_len = local_rows // blocks_dev
    is_own = owners == own_index
    ordinal = jnp.cumsum(is_own.astype(jnp.int32)) - 1
    matches = is_own[None, :] & (
        ordinal[None, :] == jnp.arange(blocks_dev, dtype=jnp.int32)[:, None]
    )
    leading = jnp.sum(
        jnp.where(matches, jnp.arange(owners.shape[0], dtype=jnp.int32)[None, :], 0), axis=1
    )
    within = jnp.arange(local_rows, dtype=jnp.int32)
    wanted = jnp.repeat(leading, block_len) * block_len + within % block_len
    portion = lax.all_gather(packed, "seq", axis=0, tiled=True)
    amount = portion.shape[0]
    choose = (wanted[:, None] == jnp.arange(amount, dtype=jnp.int32)[None, :]).astype(jnp.bfloat16)
    running = attend(
        (initial, jnp.zeros((local_rows, packed.shape[1]), jnp.float32))[0], portion, jnp.int32(0)
    )
    taken = jnp.dot(choose, portion, preferred_element_type=jnp.float32)
    kv_cache = taken.astype(jnp.bfloat16).reshape(local_rows, kv_heads, 2 * HD)
    _, running_sum, running_out = running
    attention = (
        (running_out / running_sum[..., None])
        .astype(jnp.bfloat16)
        .reshape(local_rows, query_heads * HD)
    )
    return (attention, kv_cache)


def prepare(own, lengths_ref, owners_ref, queries_ref, cos_ref, sin_ref, rotated_ref, facts_ref, slots_ref):
    local_rows, width = queries_ref.shape
    rows = own * local_rows + lax.broadcasted_iota(jnp.int32, (local_rows, HD), 0)
    positions = rows - first_rows(rows, lengths_ref)
    half = HD // 2
    lanes = lax.broadcasted_iota(jnp.int32, (local_rows, HD), 1)
    exponent = jnp.where(lanes < half, lanes, lanes - half).astype(jnp.float32) * (2.0 / HD)
    inverse = jnp.exp(-exponent * jnp.log(jnp.float32(500000.0)))
    angles = positions.astype(jnp.float32) * inverse
    cosines = jnp.cos(angles)
    sines = jnp.sin(angles)
    sines = jnp.where(lanes < half, -sines, sines)
    cos_ref[...] = cosines
    sin_ref[...] = sines
    for h in range(width // HD):
        vectors = queries_ref[:, h * HD : (h + 1) * HD].astype(jnp.float32)
        rotated_ref[:, h * HD : (h + 1) * HD] = turn(vectors, cosines, sines).astype(jnp.bfloat16)
    rows = own * local_rows + lax.broadcasted_iota(jnp.int32, (1, local_rows), 1)
    facts_ref[0:1, :] = first_rows(rows, lengths_ref)
    facts_ref[1:2, :] = rows
    facts_ref[2:3, :] = jnp.zeros_like(rows) + own
    count = jnp.int32(0)
    for b in range(owners_ref.shape[0]):
        hit = owners_ref[b] == own
        slots_ref[b] = jnp.where(hit, count, -1)
        count = count + hit.astype(jnp.int32)
    slots_ref[owners_ref.shape[0]] = own


def add_products(piece, key_ref, value_ref, sums):
    kv_width = key_ref.shape[1]
    for at, ref in ((0, key_ref), (kv_width, value_ref)):
        sums[at] = sums[at] + jnp.dot(piece, ref[...], preferred_element_type=jnp.float32)


def early_body(offsets, place_ref, key_hbm, value_hbm, own_hbm, queries_hbm, lengths_hbm, owners_hbm, *refs):
    near_refs = refs[: len(offsets) - 1]
    outs = refs[len(offsets) - 1 :]
    keys_ref, values_ref, sums_ref = outs[:3]
    tables = outs[3:8]
    own_ref, queries_ref, lengths_ref, owners_ref, weight_sems, sems = outs[8:]
    parts, width, kv_width = keys_ref.shape
    small = [
        pltpu.make_async_copy(source, goal, sems.at[n])
        for n, (source, goal) in enumerate(
            (
                (lengths_hbm, lengths_ref),
                (owners_hbm, owners_ref),
                (queries_hbm, queries_ref),
                (own_hbm, own_ref),
            )
        )
    ]
    for copy in small:
        copy.start()
    copies = []
    order = list(offsets) + [o for o in range(parts) if o not in offsets]
    for offset in order:
        start = pl.multiple_of((place_ref[1] ^ offset) * width, width)
        pair = [
            pltpu.make_async_copy(hbm.at[pl.ds(start, width)], ref.at[offset], weight_sems.at[side, offset])
            for side, (hbm, ref) in enumerate(((key_hbm, keys_ref), (value_hbm, values_ref)))
        ]
        for copy in pair:
            copy.start()
        copies.append(pair)
    for copy in small:
        copy.wait()
    prepare(place_ref[0], lengths_ref, owners_ref, queries_ref, *tables)
    sums = {0: 0.0, kv_width: 0.0}
    pieces = [own_ref] + list(near_refs)
    for n, offset in enumerate(order):
        for copy in copies[n]:
            copy.wait()
        if n < len(offsets):
            add_products(pieces[n][...], keys_ref.at[offset], values_ref.at[offset], sums)
    for at in sums:
        sums_ref[:, at : at + kv_width] = sums[at]


def far_body(offset, start, keys_ref, values_ref, sums_ref, piece_ref, out_ref):
    size = piece_ref.shape[0]
    kv_width = keys_ref.shape[2]
    rows = slice(start, start + size)
    sums = {at: sums_ref[rows, at : at + kv_width] for at in (0, kv_width)}
    add_products(piece_ref[...], keys_ref.at[offset], values_ref.at[offset], sums)
    for at in sums:
        out_ref[:, at : at + kv_width] = sums[at]


def late_body(offsets, start, keys_ref, values_ref, sums_ref, cos_ref, sin_ref, *refs):
    *refs, packed_ref = refs
    size = packed_ref.shape[0]
    kv_width = keys_ref.shape[2]
    rows = slice(start, start + size)
    sums = {at: sums_ref[:, at : at + kv_width] for at in (0, kv_width)}
    for offset, ref in zip(offsets, refs):
        add_products(ref[...], keys_ref.at[offset], values_ref.at[offset], sums)
    cosines = cos_ref[rows, :]
    sines = sin_ref[rows, :]
    for h in range(kv_width // HD):
        part = slice(h * HD, (h + 1) * HD)
        base = 2 * h * HD
        both = (turn(sums[0][:, part], cosines, sines), sums[kv_width][:, part])
        for side, block in enumerate(both):
            goal = slice(base + side * HD, base + (side + 1) * HD)
            block = block.astype(jnp.bfloat16)
            packed_ref[:, goal] = block


def attend_body(held, block_len, carried, final, facts_ref, slots_hbm, rotated_ref, *refs):
    local_rows, width = rotated_ref.shape
    parts = refs[: len(held)]
    rest = refs[len(held) :]
    old = rest[:4] if carried else ()
    rest = rest[len(old) :]
    slots_ref, slots_sem = rest[-2:]
    cache_ref = rest[-3]
    fetch = pltpu.make_async_copy(slots_hbm, slots_ref, slots_sem)
    fetch.start()
    amount = sum(ref.shape[0] for ref in parts)
    order = lax.broadcasted_iota(jnp.int32, (amount, local_rows), 0)
    own = facts_ref[2:3, :]
    key_rows = order
    at = 0
    for segments in held:
        for k, first, size in segments:
            moved = order + ((own ^ k) * local_rows + (first - at))
            key_rows = jnp.where(order >= at, moved, key_rows) if at else moved
            at += size
    allowed = (key_rows >= facts_ref[0:1, :]) & (key_rows <= facts_ref[1:2, :])
    scale = float(HD**-0.5 * np.log2(np.e))
    kv_heads = parts[0].shape[1] // (2 * HD)
    query_heads = width // HD
    group_size = query_heads // kv_heads
    if final:
        lines = lax.broadcasted_iota(jnp.int32, (local_rows, local_rows), 0)
        lanes = lax.broadcasted_iota(jnp.int32, (local_rows, local_rows), 1)
        identity = (lines == lanes).astype(jnp.bfloat16)
    keys = []
    values = []
    for j in range(kv_heads):
        base = 2 * j * HD
        keys.append(jnp.concatenate([ref[:, base : base + HD] for ref in parts], axis=0))
        value = jnp.concatenate([ref[:, base + HD : base + 2 * HD] for ref in parts], axis=0)
        values.append(value.T)
    for at in (0,):
        some = range(query_heads)
        parts_of = [slice(h * HD, (h + 1) * HD) for h in some]
        scores = [
            lax.dot_general(
                keys[h // group_size],
                rotated_ref[:, part],
                (((1,), (1,)), ((), ())),
                preferred_element_type=jnp.float32,
            )
            for h, part in zip(some, parts_of)
        ]
        if carried:
            old_tops = [old[0][h : h + 1, :] for h in some]
            old_totals = [old[1][h : h + 1, :] for h in some]
            old_outs = [old[2][part, :] for part in parts_of]
        scores = [jnp.where(allowed, score, LOW) for score in scores]
        tops = [jnp.max(score, axis=0, keepdims=True) for score in scores]
        if carried:
            tops = [jnp.maximum(top, past) for top, past in zip(tops, old_tops)]
        weights = [jnp.exp2((score - top) * scale) for score, top in zip(scores, tops)]
        totals = [jnp.sum(weight, axis=0, keepdims=True) for weight in weights]
        outs = [
            jnp.dot(
                values[h // group_size],
                weight.astype(jnp.bfloat16),
                preferred_element_type=jnp.float32,
            )
            for h, weight in zip(some, weights)
        ]
        if carried:
            factors = [jnp.exp2((past - top) * scale) for top, past in zip(tops, old_tops)]
            totals = [t + past * f for t, past, f in zip(totals, old_totals, factors)]
            outs = [out + past * f for out, past, f in zip(outs, old_outs, factors)]
        if final:
            outs = [(out * (1.0 / total)).astype(jnp.bfloat16) for out, total in zip(outs, totals)]
            for part, out in zip(parts_of, outs):
                rest[0][:, part] = lax.dot_general(
                    identity,
                    out,
                    (((1,), (1,)), ((), ())),
                    preferred_element_type=jnp.float32,
                ).astype(jnp.bfloat16)
        else:
            for h, part, top, total, out in zip(some, parts_of, tops, totals, outs):
                rest[0][h : h + 1, :] = top
                rest[1][h : h + 1, :] = total
                rest[2][part, :] = out
    if carried:
        cache_ref[...] = old[3][...]
    fetch.wait()
    own = slots_ref[slots_ref.shape[0] - 1]
    blocks_dev = local_rows // block_len
    for segments, ref in zip(held, parts):
        before = 0
        for k, first, length in segments:
            at = 0
            while at < length:
                row = first + at
                size = min(block_len - row % block_len, length - at)
                slot = slots_ref[(own ^ k) * blocks_dev + row // block_len]

                @pl.when(slot >= 0)
                def _(ref=ref, at=before + at, row=row, size=size, slot=slot):
                    goal = pl.multiple_of(slot * block_len + row % block_len, 16)
                    block = ref[at : at + size, :]
                    cache_ref[pl.ds(goal, size)] = block.reshape((size,) + cache_ref.shape[1:])

                at += size
            before += length


def join_body(*refs):
    at = 0
    for ref in refs[:-1]:
        refs[-1][at : at + ref.shape[0], :] = ref[...]
        at += ref.shape[0]


def chunked_device(activations, queries, key_weight, value_weight, lengths, owners, sizes):
    local_rows, width = activations.shape
    devices = lax.axis_size("seq")
    parts = lax.axis_size("tp")
    kv_width = key_weight.shape[1]
    place = jnp.stack([lax.axis_index("seq"), lax.axis_index("tp")]).astype(jnp.int32)
    starts = [sum(sizes[:c]) for c in range(len(sizes))]
    far = parts // 2

    def spread_over(pieces, distance):
        while distance:
            for offset in list(pieces):
                pieces[offset ^ distance] = swap(pieces[offset], "tp", distance)
            distance //= 2
        return pieces

    crossed = []
    stays = [
        pltpu.with_memory_space_constraint(a, pltpu.HBM)
        for a in (key_weight, value_weight, activations, queries, lengths, owners)
    ]
    for start, size in zip(starts, sizes):
        piece = activations[start : start + size]
        crossed.append(swap(piece, "tp", far))
    near = spread_over({0: activations}, far // 2)

    offsets = sorted(near)
    table = jax.ShapeDtypeStruct((local_rows, HD), jnp.float32)
    weights = jax.ShapeDtypeStruct((parts, width, kv_width), jnp.bfloat16)
    keys, values, sums, cosines, sines, rotated, facts, slots = call(
        functools.partial(early_body, offsets),
        [
            weights,
            weights,
            jax.ShapeDtypeStruct((local_rows, 2 * kv_width), jnp.float32),
            table,
            table,
            jax.ShapeDtypeStruct(queries.shape, queries.dtype),
            jax.ShapeDtypeStruct((8, local_rows), jnp.int32),
            jax.ShapeDtypeStruct((owners.shape[0] + 1,), jnp.int32),
        ],
        [SMEM] + [ANY] * 6 + [VMEM] * (len(offsets) - 1),
        scratch=[
            pltpu.VMEM(activations.shape, activations.dtype),
            pltpu.VMEM(queries.shape, queries.dtype),
            pltpu.SMEM(lengths.shape, jnp.int32),
            pltpu.SMEM(owners.shape, jnp.int32),
            pltpu.SemaphoreType.DMA((2, parts)),
            pltpu.SemaphoreType.DMA((4,)),
        ],
        out_specs=[VMEM] * 7 + [SMEM],
    )(place, *stays, *[near[o] for o in offsets[1:]])

    arrived = []
    ready = sums
    for piece, start, size in zip(crossed, starts, sizes):
        piece = lax.optimization_barrier((piece, ready))[0]
        late = spread_over({far: piece}, far // 2)
        del late[far]
        partial = call(
            functools.partial(far_body, far, start),
            jax.ShapeDtypeStruct((size, 2 * kv_width), jnp.float32),
            [VMEM] * 4,
        )(keys, values, sums, piece)
        offsets = sorted(late)
        packed = call(
            functools.partial(late_body, offsets, start),
            jax.ShapeDtypeStruct((size, 2 * kv_width), jnp.bfloat16),
            [VMEM] * (5 + len(offsets)),
        )(keys, values, partial, cosines, sines, *[late[o] for o in offsets])
        ready = packed
        arrived.append(packed)

    def spread(block, k):
        return swap(block, "seq", k)

    (first_at, second_at), (first_size, second_size) = starts, sizes
    mine, mine_too = arrived
    across = spread(mine, 2)
    across_too = spread(mine_too, 2)
    joined = call(
        join_body, jax.ShapeDtypeStruct((local_rows, 2 * kv_width), jnp.bfloat16), [VMEM] * 2
    )(across, mine_too)
    near_by = spread(mine, 1)
    beside = spread(joined, 1)
    opposite = spread(mine_too, 3)
    blocks = {
        "a": (mine, ((0, first_at, first_size),)),
        "b": (mine_too, ((0, second_at, second_size),)),
        "c": (across, ((2, first_at, first_size),)),
        "d": (across_too, ((2, second_at, second_size),)),
        "e": (beside, ((3, first_at, first_size), (1, second_at, second_size))),
        "g": (near_by, ((1, first_at, first_size),)),
        "f": (opposite, ((3, second_at, second_size),)),
    }
    stages = STAGES
    state = ()
    block_len = local_rows * devices // owners.shape[0]
    cache = jax.ShapeDtypeStruct((local_rows, kv_width // HD, 2 * HD), jnp.bfloat16)
    query_width = queries.shape[1]
    line = jax.ShapeDtypeStruct((query_width // HD, local_rows), jnp.float32)
    for n, held in enumerate(stages):
        final = n == len(stages) - 1
        taken = [blocks[name][0] for name in held]
        held = [blocks[name][1] for name in held]
        if final:
            results = [jax.ShapeDtypeStruct(queries.shape, jnp.bfloat16)]
        else:
            results = [line, line, jax.ShapeDtypeStruct((query_width, local_rows), jnp.float32)]
        state = call(
            functools.partial(attend_body, held, block_len, n > 0, final),
            results + [cache],
            [VMEM, ANY] + [VMEM] * (1 + len(taken) + len(state)),
            scratch=[pltpu.SMEM(slots.shape, jnp.int32), pltpu.SemaphoreType.DMA],
        )(facts, slots, rotated, *taken, *state)
    return state


def chunk_sizes(local_rows, block_len):
    first = max(1, local_rows // block_len * SHARE // 4) * block_len
    return [first, local_rows - first]


def per_device(activations, queries, key_weight, value_weight, lengths, owners):
    local_rows = activations.shape[0]
    devices = lax.axis_size("seq")
    parts = lax.axis_size("tp")
    blocks_dev = owners.shape[0] // devices
    block_len = local_rows // blocks_dev
    few = devices == 4 and 1 < parts <= 8 and is_power(parts)
    if not few or block_len % 16 or blocks_dev < 2:
        return gathered_device(activations, queries, key_weight, value_weight, lengths, owners)
    sizes = chunk_sizes(local_rows, block_len)
    return chunked_device(activations, queries, key_weight, value_weight, lengths, owners, sizes)


def solution(mesh):
    rows = P(("groups", "seq"), "tp")
    columns = P(None, "tp")

    return jax.shard_map(
        per_device,
        mesh=mesh,
        in_specs=(rows, rows, columns, columns, P("groups"), P("groups")),
        out_specs=(rows, P(("groups", "seq"), "tp", None)),
        check_vma=False,
    )
```

```python
import functools

import jax
import jax.numpy as jnp
import numpy as np
from jax import lax
from jax.experimental import pallas as pl
from jax.experimental.pallas import tpu as pltpu
from jax.sharding import PartitionSpec as P

HD = 128
LOW = -1e30
SHARE = 2
STAGES = ('acg', 'bf', 'd', 'e')
GATE = True
MIB = 1 << 20
VMEM = pl.BlockSpec(memory_space=pltpu.VMEM)
SMEM = pl.BlockSpec(memory_space=pltpu.SMEM)
ANY = pl.BlockSpec(memory_space=pltpu.HBM)


def locate(row_ids, lengths):
    prompt_ends = jnp.cumsum(lengths)
    prompt_starts = prompt_ends - lengths
    segment = jnp.sum((row_ids[:, None] >= prompt_ends[None, :]).astype(jnp.int32), axis=1)
    numbers = jnp.arange(lengths.shape[0], dtype=jnp.int32)
    prompt_first = jnp.sum(
        jnp.where(segment[:, None] == numbers[None, :], prompt_starts[None, :], 0), axis=1
    )
    return (segment, row_ids - prompt_first)


def rotate(vectors, positions):
    half_size = vectors.shape[-1] // 2
    exponent = jnp.arange(half_size, dtype=jnp.float32) * (2.0 / vectors.shape[-1])
    inverse = jnp.exp(-exponent * jnp.log(jnp.float32(500000.0)))
    angles = positions.astype(jnp.float32)[:, None] * inverse[None, :]
    cosines = jnp.cos(angles)[:, None, :]
    sine_values = jnp.sin(angles)[:, None, :]
    lower_half = vectors[..., :half_size]
    upper_half = vectors[..., half_size:]
    return jnp.concatenate(
        [
            lower_half * cosines - upper_half * sine_values,
            upper_half * cosines + lower_half * sine_values,
        ],
        axis=-1,
    )


def swap(array, axis, distance):
    count = lax.axis_size(axis)
    return lax.ppermute(array, axis, [(i, i ^ distance) for i in range(count)])


def is_power(count):
    return count & (count - 1) == 0


def call(body, out_shape, in_specs, vmem=8 * MIB, scratch=(), out_specs=None, aliases={}):
    multiple = isinstance(out_shape, (list, tuple))
    return pl.pallas_call(
        body,
        out_shape=out_shape,
        in_specs=in_specs,
        out_specs=out_specs or ([VMEM] * len(out_shape) if multiple else VMEM),
        scratch_shapes=list(scratch),
        input_output_aliases=aliases,
        compiler_params=pltpu.CompilerParams(vmem_limit_bytes=vmem),
    )


def first_rows(rows, lengths_ref):
    first = jnp.zeros_like(rows)
    start = jnp.int32(0)
    for p in range(lengths_ref.shape[0]):
        first = jnp.where(rows >= start, start, first)
        start = start + lengths_ref[p]
    return first


def turn(vectors, cosines, sines):
    return vectors * cosines + pltpu.roll(vectors, HD // 2, 1) * sines


def gathered_device(activations, queries, key_weight, value_weight, lengths, owners):
    local_rows = activations.shape[0]
    devices = lax.axis_size("seq")
    own_index = lax.axis_index("seq")
    kv_width = key_weight.shape[1]
    kv_heads = kv_width // HD
    query_heads = queries.shape[1] // HD
    group_size = query_heads // kv_heads
    row_ids = own_index * local_rows + jnp.arange(local_rows, dtype=jnp.int32)
    segment, positions = locate(row_ids, lengths)
    portion = lax.all_gather(activations, "tp", axis=1, tiled=True)
    key_rows = key_weight
    key_sums = jnp.dot(portion, key_rows, preferred_element_type=jnp.float32)
    value_sums = jnp.dot(portion, value_weight, preferred_element_type=jnp.float32)
    keys_local = rotate(key_sums.reshape(local_rows, kv_heads, HD), positions).astype(jnp.bfloat16)
    values_local = value_sums.astype(jnp.bfloat16).reshape(local_rows, kv_heads, HD)
    packed = jnp.concatenate([keys_local, values_local], axis=-1).reshape(
        local_rows, kv_heads * 2 * HD
    )
    rotated = rotate(queries.astype(jnp.float32).reshape(local_rows, query_heads, HD), positions)
    rotated = rotated.astype(jnp.bfloat16).reshape(local_rows, kv_heads, group_size, HD)

    def attend_block(running, portion, offset):
        running_max, running_sum, running_out = running
        amount = portion.shape[0]
        paired = portion.reshape(amount, kv_heads, 2 * HD)
        key_part = paired[:, :, :HD]
        value_part = paired[:, :, HD:]
        key_rows = offset + jnp.arange(amount, dtype=jnp.int32)
        key_segment, _ = locate(key_rows, lengths)
        allowed = (
            (key_segment[None, :] == segment[:, None])
            & (key_rows[None, :] <= row_ids[:, None])
            & (key_rows[None, :] >= 0)
        )
        allowed = allowed[:, None, None, :]
        scores = jnp.einsum(
            "qhgd,khd->qhgk", rotated, key_part, preferred_element_type=jnp.float32
        ) / jnp.sqrt(jnp.float32(HD))
        new_max = jnp.maximum(running_max, jnp.max(jnp.where(allowed, scores, -1e30), axis=-1))
        weights = jnp.where(allowed, jnp.exp(scores - new_max[..., None]), 0.0)
        factor = jnp.exp(running_max - new_max)
        running_sum = running_sum * factor + jnp.sum(weights, axis=-1)
        running_out = running_out * factor[..., None] + jnp.einsum(
            "qhgk,khd->qhgd",
            weights.astype(jnp.bfloat16),
            value_part,
            preferred_element_type=jnp.float32,
        )
        return (new_max, running_sum, running_out)

    def attend(running, portion, offset):
        amount = portion.shape[0]
        if amount > 512 and amount % 512 == 0:

            def advance(carried, entry):
                sub_portion, sub_offset = entry
                return (attend_block(carried, sub_portion, offset + sub_offset), None)

            offsets = jnp.arange(amount // 512, dtype=jnp.int32) * 512
            running, _ = lax.scan(
                advance, running, (portion.reshape(amount // 512, 512, portion.shape[1]), offsets)
            )
            return running
        return attend_block(running, portion, offset)

    initial = (
        jnp.full((local_rows, kv_heads, group_size), -1e30, jnp.float32),
        jnp.zeros((local_rows, kv_heads, group_size), jnp.float32),
        jnp.zeros((local_rows, kv_heads, group_size, HD), jnp.float32),
    )
    blocks_dev = owners.shape[0] // devices
    block_len = local_rows // blocks_dev
    is_own = owners == own_index
    ordinal = jnp.cumsum(is_own.astype(jnp.int32)) - 1
    matches = is_own[None, :] & (
        ordinal[None, :] == jnp.arange(blocks_dev, dtype=jnp.int32)[:, None]
    )
    leading = jnp.sum(
        jnp.where(matches, jnp.arange(owners.shape[0], dtype=jnp.int32)[None, :], 0), axis=1
    )
    within = jnp.arange(local_rows, dtype=jnp.int32)
    wanted = jnp.repeat(leading, block_len) * block_len + within % block_len
    portion = lax.all_gather(packed, "seq", axis=0, tiled=True)
    amount = portion.shape[0]
    choose = (wanted[:, None] == jnp.arange(amount, dtype=jnp.int32)[None, :]).astype(jnp.bfloat16)
    running = attend(
        (initial, jnp.zeros((local_rows, packed.shape[1]), jnp.float32))[0], portion, jnp.int32(0)
    )
    taken = jnp.dot(choose, portion, preferred_element_type=jnp.float32)
    kv_cache = taken.astype(jnp.bfloat16).reshape(local_rows, kv_heads, 2 * HD)
    _, running_sum, running_out = running
    attention = (
        (running_out / running_sum[..., None])
        .astype(jnp.bfloat16)
        .reshape(local_rows, query_heads * HD)
    )
    return (attention, kv_cache)


def prepare(own, lengths_ref, owners_ref, queries_ref, cos_ref, sin_ref, rotated_ref, facts_ref, slots_ref):
    local_rows, width = queries_ref.shape
    rows = own * local_rows + lax.broadcasted_iota(jnp.int32, (local_rows, HD), 0)
    positions = rows - first_rows(rows, lengths_ref)
    half = HD // 2
    lanes = lax.broadcasted_iota(jnp.int32, (local_rows, HD), 1)
    exponent = jnp.where(lanes < half, lanes, lanes - half).astype(jnp.float32) * (2.0 / HD)
    inverse = jnp.exp(-exponent * jnp.log(jnp.float32(500000.0)))
    angles = positions.astype(jnp.float32) * inverse
    cosines = jnp.cos(angles)
    sines = jnp.sin(angles)
    sines = jnp.where(lanes < half, -sines, sines)
    cos_ref[...] = cosines
    sin_ref[...] = sines
    for h in range(width // HD):
        vectors = queries_ref[:, h * HD : (h + 1) * HD].astype(jnp.float32)
        rotated_ref[:, h * HD : (h + 1) * HD] = turn(vectors, cosines, sines).astype(jnp.bfloat16)
    rows = own * local_rows + lax.broadcasted_iota(jnp.int32, (1, local_rows), 1)
    facts_ref[0:1, :] = first_rows(rows, lengths_ref)
    facts_ref[1:2, :] = rows
    facts_ref[2:3, :] = jnp.zeros_like(rows) + own
    count = jnp.int32(0)
    for b in range(owners_ref.shape[0]):
        hit = owners_ref[b] == own
        slots_ref[b] = jnp.where(hit, count, -1)
        count = count + hit.astype(jnp.int32)
    slots_ref[owners_ref.shape[0]] = own


def add_products(piece, key_ref, value_ref, sums):
    kv_width = key_ref.shape[1]
    for at, ref in ((0, key_ref), (kv_width, value_ref)):
        sums[at] = sums[at] + jnp.dot(piece, ref[...], preferred_element_type=jnp.float32)


def bring(place_ref, offsets, sources, goals, sems):
    pairs = []
    for n, offset in enumerate(offsets):
        width = goals[0].shape[1]
        start = pl.multiple_of((place_ref[1] ^ offset) * width, width)
        pair = [
            pltpu.make_async_copy(source.at[pl.ds(start, width)], goal.at[n], sems.at[side, n])
            for side, (source, goal) in enumerate(zip(sources, goals))
        ]
        for copy in pair:
            copy.start()
        pairs.append(pair)
    return pairs


def ahead_body(offsets, place_ref, key_hbm, value_hbm, queries_hbm, lengths_hbm, owners_hbm, *refs):
    keys_ref, values_ref = refs[:2]
    tables = refs[2:7]
    queries_ref, lengths_ref, owners_ref, weight_sems, sems = refs[7:]
    small = [
        pltpu.make_async_copy(source, goal, sems.at[n])
        for n, (source, goal) in enumerate(
            ((lengths_hbm, lengths_ref), (owners_hbm, owners_ref), (queries_hbm, queries_ref))
        )
    ]
    for copy in small:
        copy.start()
    pairs = bring(place_ref, offsets, (key_hbm, value_hbm), (keys_ref, values_ref), weight_sems)
    for copy in small:
        copy.wait()
    prepare(place_ref[0], lengths_ref, owners_ref, queries_ref, *tables)
    for pair in pairs:
        for copy in pair:
            copy.wait()


def early_body(offsets, place_ref, key_hbm, value_hbm, own_hbm, near_keys_ref, near_values_ref, *refs):
    *near_refs, keys_ref, values_ref, sums_ref, own_ref, weight_sems, own_sem = refs
    kv_width = keys_ref.shape[2]
    own_copy = pltpu.make_async_copy(own_hbm, own_ref, own_sem)
    own_copy.start()
    pairs = bring(place_ref, offsets, (key_hbm, value_hbm), (keys_ref, values_ref), weight_sems)
    sums = {0: 0.0, kv_width: 0.0}
    for n, ref in reversed(list(enumerate([own_ref] + near_refs))):
        if n == 0:
            own_copy.wait()
        add_products(ref[...], near_keys_ref.at[n], near_values_ref.at[n], sums)
    for at in sums:
        sums_ref[:, at : at + kv_width] = sums[at]
    for pair in pairs:
        for copy in pair:
            copy.wait()


def far_body(start, keys_ref, values_ref, sums_ref, piece_ref, out_ref):
    size = piece_ref.shape[0]
    kv_width = keys_ref.shape[2]
    rows = slice(start, start + size)
    sums = {at: sums_ref[rows, at : at + kv_width] for at in (0, kv_width)}
    add_products(piece_ref[...], keys_ref.at[0], values_ref.at[0], sums)
    for at in sums:
        out_ref[:, at : at + kv_width] = sums[at]


def late_body(start, keys_ref, values_ref, sums_ref, cos_ref, sin_ref, *refs):
    *refs, packed_ref = refs
    size = packed_ref.shape[0]
    kv_width = keys_ref.shape[2]
    rows = slice(start, start + size)
    sums = {at: sums_ref[:, at : at + kv_width] for at in (0, kv_width)}
    for n, ref in enumerate(refs):
        add_products(ref[...], keys_ref.at[n + 1], values_ref.at[n + 1], sums)
    cosines = cos_ref[rows, :]
    sines = sin_ref[rows, :]
    for h in range(kv_width // HD):
        part = slice(h * HD, (h + 1) * HD)
        base = 2 * h * HD
        both = (turn(sums[0][:, part], cosines, sines), sums[kv_width][:, part])
        for side, block in enumerate(both):
            goal = slice(base + side * HD, base + (side + 1) * HD)
            block = block.astype(jnp.bfloat16)
            packed_ref[:, goal] = block


def attend_body(held, block_len, carried, final, facts_ref, slots_hbm, rotated_ref, *refs):
    local_rows, width = rotated_ref.shape
    parts = refs[: len(held)]
    rest = refs[len(held) :]
    old = rest[:4] if carried else ()
    rest = rest[len(old) :]
    slots_ref, slots_sem = rest[-2:]
    cache_ref = rest[-3]
    fetch = pltpu.make_async_copy(slots_hbm, slots_ref, slots_sem)
    fetch.start()
    amount = sum(ref.shape[0] for ref in parts)
    order = lax.broadcasted_iota(jnp.int32, (amount, local_rows), 0)
    own = facts_ref[2:3, :]
    key_rows = order
    at = 0
    for segments in held:
        for k, first, size in segments:
            moved = order + ((own ^ k) * local_rows + (first - at))
            key_rows = jnp.where(order >= at, moved, key_rows) if at else moved
            at += size
    allowed = (key_rows >= facts_ref[0:1, :]) & (key_rows <= facts_ref[1:2, :])
    scale = float(HD**-0.5 * np.log2(np.e))
    kv_heads = parts[0].shape[1] // (2 * HD)
    query_heads = width // HD
    group_size = query_heads // kv_heads
    if final:
        lines = lax.broadcasted_iota(jnp.int32, (local_rows, local_rows), 0)
        lanes = lax.broadcasted_iota(jnp.int32, (local_rows, local_rows), 1)
        identity = (lines == lanes).astype(jnp.bfloat16)
    keys = []
    values = []
    for j in range(kv_heads):
        base = 2 * j * HD
        keys.append(jnp.concatenate([ref[:, base : base + HD] for ref in parts], axis=0))
        value = jnp.concatenate([ref[:, base + HD : base + 2 * HD] for ref in parts], axis=0)
        values.append(value.T)
    for at in (0,):
        some = range(query_heads)
        parts_of = [slice(h * HD, (h + 1) * HD) for h in some]
        scores = [
            lax.dot_general(
                keys[h // group_size],
                rotated_ref[:, part],
                (((1,), (1,)), ((), ())),
                preferred_element_type=jnp.float32,
            )
            for h, part in zip(some, parts_of)
        ]
        if carried:
            old_tops = [old[0][h : h + 1, :] for h in some]
            old_totals = [old[1][h : h + 1, :] for h in some]
            old_outs = [old[2][part, :] for part in parts_of]
        scores = [jnp.where(allowed, score, LOW) for score in scores]
        tops = [jnp.max(score, axis=0, keepdims=True) for score in scores]
        if carried:
            tops = [jnp.maximum(top, past) for top, past in zip(tops, old_tops)]
        weights = [jnp.exp2((score - top) * scale) for score, top in zip(scores, tops)]
        totals = [jnp.sum(weight, axis=0, keepdims=True) for weight in weights]
        outs = [
            jnp.dot(
                values[h // group_size],
                weight.astype(jnp.bfloat16),
                preferred_element_type=jnp.float32,
            )
            for h, weight in zip(some, weights)
        ]
        if carried:
            factors = [jnp.exp2((past - top) * scale) for top, past in zip(tops, old_tops)]
            totals = [t + past * f for t, past, f in zip(totals, old_totals, factors)]
            outs = [out + past * f for out, past, f in zip(outs, old_outs, factors)]
        if final:
            outs = [(out * (1.0 / total)).astype(jnp.bfloat16) for out, total in zip(outs, totals)]
            for part, out in zip(parts_of, outs):
                rest[0][:, part] = lax.dot_general(
                    identity,
                    out,
                    (((1,), (1,)), ((), ())),
                    preferred_element_type=jnp.float32,
                ).astype(jnp.bfloat16)
        else:
            for h, part, top, total, out in zip(some, parts_of, tops, totals, outs):
                rest[0][h : h + 1, :] = top
                rest[1][h : h + 1, :] = total
                rest[2][part, :] = out
    if carried:
        cache_ref[...] = old[3][...]
    fetch.wait()
    own = slots_ref[slots_ref.shape[0] - 1]
    blocks_dev = local_rows // block_len
    for segments, ref in zip(held, parts):
        before = 0
        for k, first, length in segments:
            at = 0
            while at < length:
                row = first + at
                size = min(block_len - row % block_len, length - at)
                slot = slots_ref[(own ^ k) * blocks_dev + row // block_len]

                @pl.when(slot >= 0)
                def _(ref=ref, at=before + at, row=row, size=size, slot=slot):
                    goal = pl.multiple_of(slot * block_len + row % block_len, 16)
                    block = ref[at : at + size, :]
                    cache_ref[pl.ds(goal, size)] = block.reshape((size,) + cache_ref.shape[1:])

                at += size
            before += length


def join_body(*refs):
    at = 0
    for ref in refs[:-1]:
        refs[-1][at : at + ref.shape[0], :] = ref[...]
        at += ref.shape[0]


def chunked_device(activations, queries, key_weight, value_weight, lengths, owners, sizes):
    local_rows, width = activations.shape
    devices = lax.axis_size("seq")
    parts = lax.axis_size("tp")
    kv_width = key_weight.shape[1]
    place = jnp.stack([lax.axis_index("seq"), lax.axis_index("tp")]).astype(jnp.int32)
    starts = [sum(sizes[:c]) for c in range(len(sizes))]
    far = parts // 2

    def spread_over(pieces, distance):
        while distance:
            for offset in list(pieces):
                pieces[offset ^ distance] = swap(pieces[offset], "tp", distance)
            distance //= 2
        return pieces

    crossed = []
    stays = [
        pltpu.with_memory_space_constraint(a, pltpu.HBM)
        for a in (key_weight, value_weight, activations, queries, lengths, owners)
    ]
    near_offsets = list(range(far))
    far_offsets = list(range(far, parts))
    table = jax.ShapeDtypeStruct((local_rows, HD), jnp.float32)
    weights = jax.ShapeDtypeStruct((far, width, kv_width), jnp.bfloat16)
    near_keys, near_values, cosines, sines, rotated, facts, slots = call(
        functools.partial(ahead_body, near_offsets),
        [
            weights,
            weights,
            table,
            table,
            jax.ShapeDtypeStruct(queries.shape, queries.dtype),
            jax.ShapeDtypeStruct((8, local_rows), jnp.int32),
            jax.ShapeDtypeStruct((owners.shape[0] + 1,), jnp.int32),
        ],
        [SMEM] + [ANY] * 5,
        scratch=[
            pltpu.VMEM(queries.shape, queries.dtype),
            pltpu.SMEM(lengths.shape, jnp.int32),
            pltpu.SMEM(owners.shape, jnp.int32),
            pltpu.SemaphoreType.DMA((2, far)),
            pltpu.SemaphoreType.DMA((3,)),
        ],
        out_specs=[VMEM] * 6 + [SMEM],
    )(place, *stays[:2], *stays[3:])
    for c, (start, size) in enumerate(zip(starts, sizes)):
        piece = activations[start : start + size]
        if c and GATE:
            piece = lax.optimization_barrier((piece, cosines))[0]
        crossed.append(swap(piece, "tp", far))
    near = spread_over({0: activations}, far // 2)
    keys, values, sums = call(
        functools.partial(early_body, far_offsets),
        [weights, weights, jax.ShapeDtypeStruct((local_rows, 2 * kv_width), jnp.float32)],
        [SMEM] + [ANY] * 3 + [VMEM] * (len(near_offsets) + 1),
        scratch=[
            pltpu.VMEM(activations.shape, activations.dtype),
            pltpu.SemaphoreType.DMA((2, far)),
            pltpu.SemaphoreType.DMA,
        ],
    )(place, *stays[:3], near_keys, near_values, *[near[o] for o in near_offsets[1:]])

    arrived = []
    ready = sums
    for piece, start, size in zip(crossed, starts, sizes):
        piece = lax.optimization_barrier((piece, ready))[0]
        late = spread_over({far: piece}, far // 2)
        del late[far]
        partial = call(
            functools.partial(far_body, start),
            jax.ShapeDtypeStruct((size, 2 * kv_width), jnp.float32),
            [VMEM] * 4,
        )(keys, values, sums, piece)
        offsets = sorted(late)
        packed = call(
            functools.partial(late_body, start),
            jax.ShapeDtypeStruct((size, 2 * kv_width), jnp.bfloat16),
            [VMEM] * (5 + len(offsets)),
        )(keys, values, partial, cosines, sines, *[late[o] for o in offsets])
        ready = packed
        arrived.append(packed)

    def spread(block, k):
        return swap(block, "seq", k)

    (first_at, second_at), (first_size, second_size) = starts, sizes
    mine, mine_too = arrived
    across = spread(mine, 2)
    across_too = spread(mine_too, 2)
    joined = call(
        join_body, jax.ShapeDtypeStruct((local_rows, 2 * kv_width), jnp.bfloat16), [VMEM] * 2
    )(across, mine_too)
    near_by = spread(mine, 1)
    beside = spread(joined, 1)
    opposite = spread(mine_too, 3)
    blocks = {
        "a": (mine, ((0, first_at, first_size),)),
        "b": (mine_too, ((0, second_at, second_size),)),
        "c": (across, ((2, first_at, first_size),)),
        "d": (across_too, ((2, second_at, second_size),)),
        "e": (beside, ((3, first_at, first_size), (1, second_at, second_size))),
        "g": (near_by, ((1, first_at, first_size),)),
        "f": (opposite, ((3, second_at, second_size),)),
    }
    stages = STAGES
    state = ()
    block_len = local_rows * devices // owners.shape[0]
    cache = jax.ShapeDtypeStruct((local_rows, kv_width // HD, 2 * HD), jnp.bfloat16)
    query_width = queries.shape[1]
    line = jax.ShapeDtypeStruct((query_width // HD, local_rows), jnp.float32)
    for n, held in enumerate(stages):
        final = n == len(stages) - 1
        taken = [blocks[name][0] for name in held]
        held = [blocks[name][1] for name in held]
        if final:
            results = [jax.ShapeDtypeStruct(queries.shape, jnp.bfloat16)]
        else:
            results = [line, line, jax.ShapeDtypeStruct((query_width, local_rows), jnp.float32)]
        state = call(
            functools.partial(attend_body, held, block_len, n > 0, final),
            results + [cache],
            [VMEM, ANY] + [VMEM] * (1 + len(taken) + len(state)),
            scratch=[pltpu.SMEM(slots.shape, jnp.int32), pltpu.SemaphoreType.DMA],
        )(facts, slots, rotated, *taken, *state)
    return state


def chunk_sizes(local_rows, block_len):
    first = max(1, local_rows // block_len * SHARE // 4) * block_len
    return [first, local_rows - first]


def per_device(activations, queries, key_weight, value_weight, lengths, owners):
    local_rows = activations.shape[0]
    devices = lax.axis_size("seq")
    parts = lax.axis_size("tp")
    blocks_dev = owners.shape[0] // devices
    block_len = local_rows // blocks_dev
    few = devices == 4 and 1 < parts <= 8 and is_power(parts)
    if not few or block_len % 16 or blocks_dev < 2:
        return gathered_device(activations, queries, key_weight, value_weight, lengths, owners)
    sizes = chunk_sizes(local_rows, block_len)
    return chunked_device(activations, queries, key_weight, value_weight, lengths, owners, sizes)


def solution(mesh):
    rows = P(("groups", "seq"), "tp")
    columns = P(None, "tp")

    return jax.shard_map(
        per_device,
        mesh=mesh,
        in_specs=(rows, rows, columns, columns, P("groups"), P("groups")),
        out_specs=(rows, P(("groups", "seq"), "tp", None)),
        check_vma=False,
    )
```

```python
import functools

import jax
import jax.numpy as jnp
import numpy as np
from jax import lax
from jax.experimental import pallas as pl
from jax.experimental.pallas import tpu as pltpu
from jax.sharding import PartitionSpec as P

HD = 128
LOW = -1e30
SHARE = 5
STAGES = ('abcg', 'fd', 'e')
GATE = True
MIB = 1 << 20
VMEM = pl.BlockSpec(memory_space=pltpu.VMEM)
SMEM = pl.BlockSpec(memory_space=pltpu.SMEM)
ANY = pl.BlockSpec(memory_space=pltpu.HBM)


def locate(row_ids, lengths):
    prompt_ends = jnp.cumsum(lengths)
    prompt_starts = prompt_ends - lengths
    segment = jnp.sum((row_ids[:, None] >= prompt_ends[None, :]).astype(jnp.int32), axis=1)
    numbers = jnp.arange(lengths.shape[0], dtype=jnp.int32)
    prompt_first = jnp.sum(
        jnp.where(segment[:, None] == numbers[None, :], prompt_starts[None, :], 0), axis=1
    )
    return (segment, row_ids - prompt_first)


def rotate(vectors, positions):
    half_size = vectors.shape[-1] // 2
    exponent = jnp.arange(half_size, dtype=jnp.float32) * (2.0 / vectors.shape[-1])
    inverse = jnp.exp(-exponent * jnp.log(jnp.float32(500000.0)))
    angles = positions.astype(jnp.float32)[:, None] * inverse[None, :]
    cosines = jnp.cos(angles)[:, None, :]
    sine_values = jnp.sin(angles)[:, None, :]
    lower_half = vectors[..., :half_size]
    upper_half = vectors[..., half_size:]
    return jnp.concatenate(
        [
            lower_half * cosines - upper_half * sine_values,
            upper_half * cosines + lower_half * sine_values,
        ],
        axis=-1,
    )


def swap(array, axis, distance):
    count = lax.axis_size(axis)
    return lax.ppermute(array, axis, [(i, i ^ distance) for i in range(count)])


def is_power(count):
    return count & (count - 1) == 0


def call(body, out_shape, in_specs, vmem=8 * MIB, scratch=(), out_specs=None, aliases={}):
    multiple = isinstance(out_shape, (list, tuple))
    return pl.pallas_call(
        body,
        out_shape=out_shape,
        in_specs=in_specs,
        out_specs=out_specs or ([VMEM] * len(out_shape) if multiple else VMEM),
        scratch_shapes=list(scratch),
        input_output_aliases=aliases,
        compiler_params=pltpu.CompilerParams(vmem_limit_bytes=vmem),
    )


def first_rows(rows, lengths_ref):
    first = jnp.zeros_like(rows)
    start = jnp.int32(0)
    for p in range(lengths_ref.shape[0]):
        first = jnp.where(rows >= start, start, first)
        start = start + lengths_ref[p]
    return first


def turn(vectors, cosines, sines):
    return vectors * cosines + pltpu.roll(vectors, HD // 2, 1) * sines


def gathered_device(activations, queries, key_weight, value_weight, lengths, owners):
    local_rows = activations.shape[0]
    devices = lax.axis_size("seq")
    own_index = lax.axis_index("seq")
    kv_width = key_weight.shape[1]
    kv_heads = kv_width // HD
    query_heads = queries.shape[1] // HD
    group_size = query_heads // kv_heads
    row_ids = own_index * local_rows + jnp.arange(local_rows, dtype=jnp.int32)
    segment, positions = locate(row_ids, lengths)
    portion = lax.all_gather(activations, "tp", axis=1, tiled=True)
    key_rows = key_weight
    key_sums = jnp.dot(portion, key_rows, preferred_element_type=jnp.float32)
    value_sums = jnp.dot(portion, value_weight, preferred_element_type=jnp.float32)
    keys_local = rotate(key_sums.reshape(local_rows, kv_heads, HD), positions).astype(jnp.bfloat16)
    values_local = value_sums.astype(jnp.bfloat16).reshape(local_rows, kv_heads, HD)
    packed = jnp.concatenate([keys_local, values_local], axis=-1).reshape(
        local_rows, kv_heads * 2 * HD
    )
    rotated = rotate(queries.astype(jnp.float32).reshape(local_rows, query_heads, HD), positions)
    rotated = rotated.astype(jnp.bfloat16).reshape(local_rows, kv_heads, group_size, HD)

    def attend_block(running, portion, offset):
        running_max, running_sum, running_out = running
        amount = portion.shape[0]
        paired = portion.reshape(amount, kv_heads, 2 * HD)
        key_part = paired[:, :, :HD]
        value_part = paired[:, :, HD:]
        key_rows = offset + jnp.arange(amount, dtype=jnp.int32)
        key_segment, _ = locate(key_rows, lengths)
        allowed = (
            (key_segment[None, :] == segment[:, None])
            & (key_rows[None, :] <= row_ids[:, None])
            & (key_rows[None, :] >= 0)
        )
        allowed = allowed[:, None, None, :]
        scores = jnp.einsum(
            "qhgd,khd->qhgk", rotated, key_part, preferred_element_type=jnp.float32
        ) / jnp.sqrt(jnp.float32(HD))
        new_max = jnp.maximum(running_max, jnp.max(jnp.where(allowed, scores, -1e30), axis=-1))
        weights = jnp.where(allowed, jnp.exp(scores - new_max[..., None]), 0.0)
        factor = jnp.exp(running_max - new_max)
        running_sum = running_sum * factor + jnp.sum(weights, axis=-1)
        running_out = running_out * factor[..., None] + jnp.einsum(
            "qhgk,khd->qhgd",
            weights.astype(jnp.bfloat16),
            value_part,
            preferred_element_type=jnp.float32,
        )
        return (new_max, running_sum, running_out)

    def attend(running, portion, offset):
        amount = portion.shape[0]
        if amount > 512 and amount % 512 == 0:

            def advance(carried, entry):
                sub_portion, sub_offset = entry
                return (attend_block(carried, sub_portion, offset + sub_offset), None)

            offsets = jnp.arange(amount // 512, dtype=jnp.int32) * 512
            running, _ = lax.scan(
                advance, running, (portion.reshape(amount // 512, 512, portion.shape[1]), offsets)
            )
            return running
        return attend_block(running, portion, offset)

    initial = (
        jnp.full((local_rows, kv_heads, group_size), -1e30, jnp.float32),
        jnp.zeros((local_rows, kv_heads, group_size), jnp.float32),
        jnp.zeros((local_rows, kv_heads, group_size, HD), jnp.float32),
    )
    blocks_dev = owners.shape[0] // devices
    block_len = local_rows // blocks_dev
    is_own = owners == own_index
    ordinal = jnp.cumsum(is_own.astype(jnp.int32)) - 1
    matches = is_own[None, :] & (
        ordinal[None, :] == jnp.arange(blocks_dev, dtype=jnp.int32)[:, None]
    )
    leading = jnp.sum(
        jnp.where(matches, jnp.arange(owners.shape[0], dtype=jnp.int32)[None, :], 0), axis=1
    )
    within = jnp.arange(local_rows, dtype=jnp.int32)
    wanted = jnp.repeat(leading, block_len) * block_len + within % block_len
    portion = lax.all_gather(packed, "seq", axis=0, tiled=True)
    amount = portion.shape[0]
    choose = (wanted[:, None] == jnp.arange(amount, dtype=jnp.int32)[None, :]).astype(jnp.bfloat16)
    running = attend(
        (initial, jnp.zeros((local_rows, packed.shape[1]), jnp.float32))[0], portion, jnp.int32(0)
    )
    taken = jnp.dot(choose, portion, preferred_element_type=jnp.float32)
    kv_cache = taken.astype(jnp.bfloat16).reshape(local_rows, kv_heads, 2 * HD)
    _, running_sum, running_out = running
    attention = (
        (running_out / running_sum[..., None])
        .astype(jnp.bfloat16)
        .reshape(local_rows, query_heads * HD)
    )
    return (attention, kv_cache)


def prepare(own, lengths_ref, owners_ref, queries_ref, cos_ref, sin_ref, rotated_ref, facts_ref, slots_ref):
    local_rows, width = queries_ref.shape
    rows = own * local_rows + lax.broadcasted_iota(jnp.int32, (local_rows, HD), 0)
    positions = rows - first_rows(rows, lengths_ref)
    half = HD // 2
    lanes = lax.broadcasted_iota(jnp.int32, (local_rows, HD), 1)
    exponent = jnp.where(lanes < half, lanes, lanes - half).astype(jnp.float32) * (2.0 / HD)
    inverse = jnp.exp(-exponent * jnp.log(jnp.float32(500000.0)))
    angles = positions.astype(jnp.float32) * inverse
    cosines = jnp.cos(angles)
    sines = jnp.sin(angles)
    sines = jnp.where(lanes < half, -sines, sines)
    cos_ref[...] = cosines
    sin_ref[...] = sines
    for h in range(width // HD):
        vectors = queries_ref[:, h * HD : (h + 1) * HD].astype(jnp.float32)
        rotated_ref[:, h * HD : (h + 1) * HD] = turn(vectors, cosines, sines).astype(jnp.bfloat16)
    rows = own * local_rows + lax.broadcasted_iota(jnp.int32, (1, local_rows), 1)
    facts_ref[0:1, :] = first_rows(rows, lengths_ref)
    facts_ref[1:2, :] = rows
    facts_ref[2:3, :] = jnp.zeros_like(rows) + own
    count = jnp.int32(0)
    for b in range(owners_ref.shape[0]):
        hit = owners_ref[b] == own
        slots_ref[b] = jnp.where(hit, count, -1)
        count = count + hit.astype(jnp.int32)
    slots_ref[owners_ref.shape[0]] = own


def add_products(piece, key_ref, value_ref, sums):
    kv_width = key_ref.shape[1]
    for at, ref in ((0, key_ref), (kv_width, value_ref)):
        sums[at] = sums[at] + jnp.dot(piece, ref[...], preferred_element_type=jnp.float32)


def bring(place_ref, offsets, sources, goals, sems):
    pairs = []
    for n, offset in enumerate(offsets):
        width = goals[0].shape[1]
        start = pl.multiple_of((place_ref[1] ^ offset) * width, width)
        pair = [
            pltpu.make_async_copy(source.at[pl.ds(start, width)], goal.at[n], sems.at[side, n])
            for side, (source, goal) in enumerate(zip(sources, goals))
        ]
        for copy in pair:
            copy.start()
        pairs.append(pair)
    return pairs


def ahead_body(offsets, place_ref, key_hbm, value_hbm, queries_hbm, lengths_hbm, owners_hbm, *refs):
    keys_ref, values_ref = refs[:2]
    tables = refs[2:7]
    queries_ref, lengths_ref, owners_ref, weight_sems, sems = refs[7:]
    small = [
        pltpu.make_async_copy(source, goal, sems.at[n])
        for n, (source, goal) in enumerate(
            ((lengths_hbm, lengths_ref), (owners_hbm, owners_ref), (queries_hbm, queries_ref))
        )
    ]
    for copy in small:
        copy.start()
    pairs = bring(place_ref, offsets, (key_hbm, value_hbm), (keys_ref, values_ref), weight_sems)
    for copy in small:
        copy.wait()
    prepare(place_ref[0], lengths_ref, owners_ref, queries_ref, *tables)
    for pair in pairs:
        for copy in pair:
            copy.wait()


def early_body(offsets, place_ref, key_hbm, value_hbm, own_hbm, near_keys_ref, near_values_ref, *refs):
    *near_refs, keys_ref, values_ref, sums_ref, own_ref, weight_sems, own_sem = refs
    kv_width = keys_ref.shape[2]
    own_copy = pltpu.make_async_copy(own_hbm, own_ref, own_sem)
    own_copy.start()
    pairs = bring(place_ref, offsets, (key_hbm, value_hbm), (keys_ref, values_ref), weight_sems)
    sums = {0: 0.0, kv_width: 0.0}
    for n, ref in reversed(list(enumerate([own_ref] + near_refs))):
        if n == 0:
            own_copy.wait()
        add_products(ref[...], near_keys_ref.at[n], near_values_ref.at[n], sums)
    for at in sums:
        sums_ref[:, at : at + kv_width] = sums[at]
    for pair in pairs:
        for copy in pair:
            copy.wait()


def far_body(start, keys_ref, values_ref, sums_ref, piece_ref, out_ref):
    size = piece_ref.shape[0]
    kv_width = keys_ref.shape[2]
    rows = slice(start, start + size)
    sums = {at: sums_ref[rows, at : at + kv_width] for at in (0, kv_width)}
    add_products(piece_ref[...], keys_ref.at[0], values_ref.at[0], sums)
    for at in sums:
        out_ref[:, at : at + kv_width] = sums[at]


def late_body(start, keys_ref, values_ref, sums_ref, cos_ref, sin_ref, *refs):
    *refs, packed_ref = refs
    size = packed_ref.shape[0]
    kv_width = keys_ref.shape[2]
    rows = slice(start, start + size)
    sums = {at: sums_ref[:, at : at + kv_width] for at in (0, kv_width)}
    for n, ref in enumerate(refs):
        add_products(ref[...], keys_ref.at[n + 1], values_ref.at[n + 1], sums)
    cosines = cos_ref[rows, :]
    sines = sin_ref[rows, :]
    for h in range(kv_width // HD):
        part = slice(h * HD, (h + 1) * HD)
        base = 2 * h * HD
        both = (turn(sums[0][:, part], cosines, sines), sums[kv_width][:, part])
        for side, block in enumerate(both):
            goal = slice(base + side * HD, base + (side + 1) * HD)
            block = block.astype(jnp.bfloat16)
            packed_ref[:, goal] = block


def attend_body(held, block_len, carried, final, facts_ref, slots_hbm, rotated_ref, *refs):
    local_rows, width = rotated_ref.shape
    parts = refs[: len(held)]
    rest = refs[len(held) :]
    old = rest[:4] if carried else ()
    rest = rest[len(old) :]
    slots_ref, slots_sem = rest[-2:]
    cache_ref = rest[-3]
    fetch = pltpu.make_async_copy(slots_hbm, slots_ref, slots_sem)
    fetch.start()
    amount = sum(ref.shape[0] for ref in parts)
    order = lax.broadcasted_iota(jnp.int32, (amount, local_rows), 0)
    own = facts_ref[2:3, :]
    key_rows = order
    at = 0
    for segments in held:
        for k, first, size in segments:
            moved = order + ((own ^ k) * local_rows + (first - at))
            key_rows = jnp.where(order >= at, moved, key_rows) if at else moved
            at += size
    allowed = (key_rows >= facts_ref[0:1, :]) & (key_rows <= facts_ref[1:2, :])
    scale = float(HD**-0.5 * np.log2(np.e))
    kv_heads = parts[0].shape[1] // (2 * HD)
    query_heads = width // HD
    group_size = query_heads // kv_heads
    if final:
        lines = lax.broadcasted_iota(jnp.int32, (local_rows, local_rows), 0)
        lanes = lax.broadcasted_iota(jnp.int32, (local_rows, local_rows), 1)
        identity = (lines == lanes).astype(jnp.bfloat16)
    keys = []
    values = []
    for j in range(kv_heads):
        base = 2 * j * HD
        keys.append(jnp.concatenate([ref[:, base : base + HD] for ref in parts], axis=0))
        value = jnp.concatenate([ref[:, base + HD : base + 2 * HD] for ref in parts], axis=0)
        values.append(value.T)
    for at in (0,):
        some = range(query_heads)
        parts_of = [slice(h * HD, (h + 1) * HD) for h in some]
        scores = [
            lax.dot_general(
                keys[h // group_size],
                rotated_ref[:, part],
                (((1,), (1,)), ((), ())),
                preferred_element_type=jnp.float32,
            )
            for h, part in zip(some, parts_of)
        ]
        if carried:
            old_tops = [old[0][h : h + 1, :] for h in some]
            old_totals = [old[1][h : h + 1, :] for h in some]
            old_outs = [old[2][part, :] for part in parts_of]
        scores = [jnp.where(allowed, score, LOW) for score in scores]
        tops = [jnp.max(score, axis=0, keepdims=True) for score in scores]
        if carried:
            tops = [jnp.maximum(top, past) for top, past in zip(tops, old_tops)]
        weights = [jnp.exp2((score - top) * scale) for score, top in zip(scores, tops)]
        totals = [jnp.sum(weight, axis=0, keepdims=True) for weight in weights]
        outs = [
            jnp.dot(
                values[h // group_size],
                weight.astype(jnp.bfloat16),
                preferred_element_type=jnp.float32,
            )
            for h, weight in zip(some, weights)
        ]
        if carried:
            factors = [jnp.exp2((past - top) * scale) for top, past in zip(tops, old_tops)]
            totals = [t + past * f for t, past, f in zip(totals, old_totals, factors)]
            outs = [out + past * f for out, past, f in zip(outs, old_outs, factors)]
        if final:
            outs = [(out * (1.0 / total)).astype(jnp.bfloat16) for out, total in zip(outs, totals)]
            for part, out in zip(parts_of, outs):
                rest[0][:, part] = lax.dot_general(
                    identity,
                    out,
                    (((1,), (1,)), ((), ())),
                    preferred_element_type=jnp.float32,
                ).astype(jnp.bfloat16)
        else:
            for h, part, top, total, out in zip(some, parts_of, tops, totals, outs):
                rest[0][h : h + 1, :] = top
                rest[1][h : h + 1, :] = total
                rest[2][part, :] = out
    if carried:
        cache_ref[...] = old[3][...]
    fetch.wait()
    own = slots_ref[slots_ref.shape[0] - 1]
    blocks_dev = local_rows // block_len
    for segments, ref in zip(held, parts):
        before = 0
        for k, first, length in segments:
            at = 0
            while at < length:
                row = first + at
                size = min(block_len - row % block_len, length - at)
                slot = slots_ref[(own ^ k) * blocks_dev + row // block_len]

                @pl.when(slot >= 0)
                def _(ref=ref, at=before + at, row=row, size=size, slot=slot):
                    goal = pl.multiple_of(slot * block_len + row % block_len, 16)
                    block = ref[at : at + size, :]
                    cache_ref[pl.ds(goal, size)] = block.reshape((size,) + cache_ref.shape[1:])

                at += size
            before += length


def join_body(*refs):
    at = 0
    for ref in refs[:-1]:
        refs[-1][at : at + ref.shape[0], :] = ref[...]
        at += ref.shape[0]


def chunked_device(activations, queries, key_weight, value_weight, lengths, owners, sizes):
    local_rows, width = activations.shape
    devices = lax.axis_size("seq")
    parts = lax.axis_size("tp")
    kv_width = key_weight.shape[1]
    place = jnp.stack([lax.axis_index("seq"), lax.axis_index("tp")]).astype(jnp.int32)
    starts = [sum(sizes[:c]) for c in range(len(sizes))]
    far = parts // 2

    def spread_over(pieces, distance):
        while distance:
            for offset in list(pieces):
                pieces[offset ^ distance] = swap(pieces[offset], "tp", distance)
            distance //= 2
        return pieces

    crossed = []
    stays = [
        pltpu.with_memory_space_constraint(a, pltpu.HBM)
        for a in (key_weight, value_weight, activations, queries, lengths, owners)
    ]
    near_offsets = list(range(far))
    far_offsets = list(range(far, parts))
    table = jax.ShapeDtypeStruct((local_rows, HD), jnp.float32)
    weights = jax.ShapeDtypeStruct((far, width, kv_width), jnp.bfloat16)
    near_keys, near_values, cosines, sines, rotated, facts, slots = call(
        functools.partial(ahead_body, near_offsets),
        [
            weights,
            weights,
            table,
            table,
            jax.ShapeDtypeStruct(queries.shape, queries.dtype),
            jax.ShapeDtypeStruct((8, local_rows), jnp.int32),
            jax.ShapeDtypeStruct((owners.shape[0] + 1,), jnp.int32),
        ],
        [SMEM] + [ANY] * 5,
        scratch=[
            pltpu.VMEM(queries.shape, queries.dtype),
            pltpu.SMEM(lengths.shape, jnp.int32),
            pltpu.SMEM(owners.shape, jnp.int32),
            pltpu.SemaphoreType.DMA((2, far)),
            pltpu.SemaphoreType.DMA((3,)),
        ],
        out_specs=[VMEM] * 6 + [SMEM],
    )(place, *stays[:2], *stays[3:])
    for c, (start, size) in enumerate(zip(starts, sizes)):
        piece = activations[start : start + size]
        if c and GATE:
            piece = lax.optimization_barrier((piece, cosines))[0]
        crossed.append(swap(piece, "tp", far))
    near = spread_over({0: activations}, far // 2)
    keys, values, sums = call(
        functools.partial(early_body, far_offsets),
        [weights, weights, jax.ShapeDtypeStruct((local_rows, 2 * kv_width), jnp.float32)],
        [SMEM] + [ANY] * 3 + [VMEM] * (len(near_offsets) + 1),
        scratch=[
            pltpu.VMEM(activations.shape, activations.dtype),
            pltpu.SemaphoreType.DMA((2, far)),
            pltpu.SemaphoreType.DMA,
        ],
    )(place, *stays[:3], near_keys, near_values, *[near[o] for o in near_offsets[1:]])

    arrived = []
    ready = sums
    for piece, start, size in zip(crossed, starts, sizes):
        piece = lax.optimization_barrier((piece, ready))[0]
        late = spread_over({far: piece}, far // 2)
        del late[far]
        partial = call(
            functools.partial(far_body, start),
            jax.ShapeDtypeStruct((size, 2 * kv_width), jnp.float32),
            [VMEM] * 4,
        )(keys, values, sums, piece)
        offsets = sorted(late)
        packed = call(
            functools.partial(late_body, start),
            jax.ShapeDtypeStruct((size, 2 * kv_width), jnp.bfloat16),
            [VMEM] * (5 + len(offsets)),
        )(keys, values, partial, cosines, sines, *[late[o] for o in offsets])
        ready = packed
        arrived.append(packed)

    def spread(block, k):
        return swap(block, "seq", k)

    (first_at, second_at), (first_size, second_size) = starts, sizes
    mine, mine_too = arrived
    across = spread(mine, 2)
    across_too = spread(mine_too, 2)
    joined = call(
        join_body, jax.ShapeDtypeStruct((local_rows, 2 * kv_width), jnp.bfloat16), [VMEM] * 2
    )(across, mine_too)
    near_by = spread(mine, 1)
    beside = spread(joined, 1)
    opposite = spread(mine_too, 3)
    blocks = {
        "a": (mine, ((0, first_at, first_size),)),
        "b": (mine_too, ((0, second_at, second_size),)),
        "c": (across, ((2, first_at, first_size),)),
        "d": (across_too, ((2, second_at, second_size),)),
        "e": (beside, ((3, first_at, first_size), (1, second_at, second_size))),
        "g": (near_by, ((1, first_at, first_size),)),
        "f": (opposite, ((3, second_at, second_size),)),
    }
    stages = STAGES
    state = ()
    block_len = local_rows * devices // owners.shape[0]
    cache = jax.ShapeDtypeStruct((local_rows, kv_width // HD, 2 * HD), jnp.bfloat16)
    query_width = queries.shape[1]
    line = jax.ShapeDtypeStruct((query_width // HD, local_rows), jnp.float32)
    for n, held in enumerate(stages):
        final = n == len(stages) - 1
        taken = [blocks[name][0] for name in held]
        held = [blocks[name][1] for name in held]
        if final:
            results = [jax.ShapeDtypeStruct(queries.shape, jnp.bfloat16)]
        else:
            results = [line, line, jax.ShapeDtypeStruct((query_width, local_rows), jnp.float32)]
        state = call(
            functools.partial(attend_body, held, block_len, n > 0, final),
            results + [cache],
            [VMEM, ANY] + [VMEM] * (1 + len(taken) + len(state)),
            scratch=[pltpu.SMEM(slots.shape, jnp.int32), pltpu.SemaphoreType.DMA],
        )(facts, slots, rotated, *taken, *state)
    return state


def chunk_sizes(local_rows):
    first = local_rows * SHARE // 8 // 16 * 16
    return [first, local_rows - first]


def per_device(activations, queries, key_weight, value_weight, lengths, owners):
    local_rows = activations.shape[0]
    devices = lax.axis_size("seq")
    parts = lax.axis_size("tp")
    blocks_dev = owners.shape[0] // devices
    block_len = local_rows // blocks_dev
    few = devices == 4 and 1 < parts <= 8 and is_power(parts)
    if not few or block_len % 16 or blocks_dev < 2:
        return gathered_device(activations, queries, key_weight, value_weight, lengths, owners)
    sizes = chunk_sizes(local_rows)
    return chunked_device(activations, queries, key_weight, value_weight, lengths, owners, sizes)


def solution(mesh):
    rows = P(("groups", "seq"), "tp")
    columns = P(None, "tp")

    return jax.shard_map(
        per_device,
        mesh=mesh,
        in_specs=(rows, rows, columns, columns, P("groups"), P("groups")),
        out_specs=(rows, P(("groups", "seq"), "tp", None)),
        check_vma=False,
    )
```
